32 devices in a mesh: shell: 4 (over y, x), band: 8 (over z, core).
Axes of the slice: x: 2, y: 2, z: 4, core: 2. Of those that a mesh axis runs over, the one named last changes fastest.
Arguments:
- density: float32 [8, 640, 1280], P('shell', 'band'), may hold values from -6 to 6
- momentum: float32 [8, 640, 1280], P('shell', 'band'), may hold values from -6 to 6
- observed: float32 [800, 2, 640], P('band'), may hold values from -12 to 12
- order_list: int32 [800], replicated, may hold values from 0 to 640, as said below
- shell_ratio: float32 [8], P('shell'), may hold values from 0.985 to 0.9995
- precision: float32 [640], replicated, may hold values from 0.03 to 0.3
Outputs:
- new_density: float32 [8, 640, 1280], P('shell', 'band')
- new_momentum: float32 [8, 640, 1280], P('shell', 'band')
The draws below stay inside these ranges and needn't reach their ends.
Inputs may be any that keep to these rules, and one draw needn't show every extreme that they name: `order_list`: each order 0 to 639 stands in exactly one slot; the value 640 marks an empty slot. The slots of band index d are entries d * 100 to (d + 1) * 100 - 1, live ones first; some band index has all 100 slots live.
All inputs are finite; a program needn't handle non-finite values.
Results may differ from the reference program's by a relative error of at most 0.0003.
Values sent between devices are 32-bit elements; how exact they have to be, the bound alone decides.
A program may use at most 192 MiB of HBM per device.

```python
import math
import jax
import jax.numpy as jnp
from jax import lax

DEG = 640
NLAT = 640
NLON = 1280
SHELLS = 8
SLOTS = 100
SLOTS_ALL = 800
N_BAND = 8


def draw_order_list(key, part):
    mean_count = DEG // N_BAND
    extra_count = SLOTS - mean_count
    place_key = jax.random.fold_in(key, 11)
    shift_key = jax.random.fold_in(key, 12)
    order_key = jax.random.fold_in(key, 13)
    shifts = jax.random.randint(shift_key, (N_BAND // 2,), 0, extra_count + 1)
    shifts = shifts.at[0].set(extra_count)
    signed = jnp.concatenate([shifts, -shifts])
    placed = jax.random.permutation(place_key, N_BAND)
    counts = mean_count + signed[placed]
    starts = jnp.cumsum(counts) - counts
    slot_index = jnp.arange(SLOTS)
    active = slot_index[None, :] < counts[:, None]
    chosen = jnp.minimum(starts[:, None] + slot_index[None, :], DEG - 1)
    shuffled = jax.random.permutation(order_key, DEG)
    return jnp.where(active, shuffled[chosen], DEG).reshape(-1).astype(jnp.int32)


def steps_of(stream_key, extent, pieces, least, high):
    level, own = 1.0, jax.random.fold_in(stream_key, 6)
    for axis_at, parts in pieces:
        heights = jnp.exp(jax.random.uniform(jax.random.fold_in(own, axis_at), (parts,), jnp.float32, least / len(pieces), high / len(pieces)))
        level = level * jnp.repeat(heights, extent[axis_at] // parts).reshape([-1 if axis == axis_at else 1 for axis in range(len(extent))])
    return level


def bell_draw(rng, dims, scale, reach, cuts=(), held_as=jnp.bfloat16):
    values = scale * jax.random.normal(rng, dims, jnp.float32)
    if cuts:
        values = values * steps_of(rng, dims, cuts, -0.22, 0.18)
    return jnp.clip(values, -reach, reach).astype(held_as)


def setup_inputs(seed: int = 0) -> dict:
    arg_keys = jax.random.split(jax.random.key(seed), 7)
    return {
        "density": bell_draw(arg_keys[0], (SHELLS, NLAT, NLON), 1.0, 6.0, ((0, 4), (1, 8)), jnp.float32),
        "momentum": bell_draw(arg_keys[1], (SHELLS, NLAT, NLON), 1.0, 6.0, ((0, 4), (1, 8)), jnp.float32),
        "observed": bell_draw(arg_keys[2], (SLOTS_ALL, 2, DEG), 2.0, 12.0, ((0, 8),), jnp.float32),
        "order_list": draw_order_list(jax.random.fold_in(arg_keys[6], 71), 0),
        "shell_ratio": jnp.clip(jnp.exp(math.log(0.9995) - 0.014613475 * jax.random.uniform(arg_keys[4], (SHELLS,), jnp.float32) ** steps_of(arg_keys[4], (SHELLS,), ((0, 4),), -0.2, 0.2)), 0.985, 0.9995),
        "precision": jnp.clip(jnp.exp(jax.random.uniform(arg_keys[5], (DEG,), jnp.float32, math.log(0.03), math.log(0.3))), 0.03, 0.3),
    }


STEP = 0.5
HIGH = lax.Precision.HIGHEST

def legendre_table(orders, lat_total, degrees):
    half_rows = lat_total // 2
    colatitude = (jnp.arange(half_rows, dtype=jnp.float32) + 0.5) * (jnp.pi / lat_total)
    cosine = jnp.cos(colatitude)[None, :]
    sine_row = jnp.sin(colatitude)[None, :]
    quadrature = jnp.sqrt(sine_row * (jnp.pi / lat_total))
    order_value = orders.astype(jnp.float32)[:, None]
    seed_log = order_value * jnp.log(sine_row) + 0.5 * (jnp.log(order_value + 0.5) + lax.lgamma(2.0 * order_value + 1.0) - order_value * jnp.log(4.0) - 2.0 * lax.lgamma(order_value + 1.0))
    number = orders.shape[0]
    span_rows = 64

    def one_span(position, carry):
        legendre, current, previous, scale_log = carry
        position = position.astype(jnp.int32)
        collected = []
        for offset_step in range(span_rows):
            offset = position * span_rows + offset_step
            inside = orders[:, None] + offset < degrees
            collected.append(jnp.where(inside, current * jnp.exp(scale_log) * quadrature, 0.0))
            next_step = (offset + 1).astype(jnp.float32)
            growth = jnp.sqrt((4.0 * (order_value + next_step) ** 2 - 1.0) / (next_step * (2.0 * order_value + next_step)))
            lower_sq = (order_value + next_step - 1.0) ** 2
            damping = jnp.sqrt((next_step - 1.0) * (2.0 * order_value + next_step - 1.0) / jnp.maximum(4.0 * lower_sq - 1.0, 1.0))
            current, previous = (growth * (cosine * current - damping * previous), current)
            if offset_step % 16 == 15:
                largest = jnp.maximum(jnp.abs(current), jnp.abs(previous))
                current = current / largest
                previous = previous / largest
                scale_log = scale_log + jnp.log(largest)
        rows_tile = jnp.stack(collected, axis=1).reshape(number, span_rows // 2, 2, half_rows)
        zero_index = jnp.zeros((), jnp.int32)
        legendre = lax.dynamic_update_slice(legendre, rows_tile, (zero_index, position * (span_rows // 2), zero_index, zero_index))
        return (legendre, current, previous, scale_log)
    initial = (jnp.zeros((number, degrees // 2, 2, half_rows), jnp.float32), jnp.ones((number, half_rows), jnp.float32), jnp.zeros((number, half_rows), jnp.float32), seed_log)
    return lax.fori_loop(0, degrees // span_rows, one_span, initial)[0]

def analyse(spectra, legendre):
    half_rows = spectra.shape[3] // 2
    northern = spectra[..., :half_rows]
    southern = jnp.flip(spectra[..., half_rows:], axis=3)
    folded = jnp.stack([northern + southern, northern - southern], axis=3)
    return jnp.einsum('bipz,bcspz->bcsip', legendre, folded, precision=HIGH, preferred_element_type=jnp.float32)

def synthesise(weighted, legendre):
    number, planes, shells, offsets = weighted.shape
    paired = weighted.reshape(number, planes, shells, offsets // 2, 2)
    folded = jnp.einsum('bipz,bcsip->bcspz', legendre, paired, precision=HIGH, preferred_element_type=jnp.float32)
    northern = folded[:, :, :, 0] + folded[:, :, :, 1]
    southern = jnp.flip(folded[:, :, :, 0] - folded[:, :, :, 1], axis=3)
    return jnp.concatenate([northern, southern], axis=3)

def likelihood(field_grid, observed, order_list, shell_ratio, precision):
    order_index = jnp.arange(DEG, dtype=jnp.int32)
    factor = jnp.where(order_index == 0, math.sqrt(1.0 / NLON), math.sqrt(2.0 / NLON)).astype(jnp.float32)
    spectra = jnp.fft.rfft(field_grid, axis=2)[:, :, :DEG]
    stacked = jnp.stack([jnp.real(spectra) * factor, jnp.imag(spectra) * factor])
    by_order = jnp.transpose(stacked, (3, 0, 1, 2))
    groups = jnp.arange(DEG, dtype=jnp.int32).reshape(DEG // 64, 64)

    def forward_group(group_item):
        return analyse(group_item[1], legendre_table(group_item[0], NLAT, DEG))
    shell_terms = lax.map(forward_group, (groups, by_order.reshape(DEG // 64, 64, 2, SHELLS, NLAT))).reshape(DEG, 2, SHELLS, DEG)
    degree_grid = (order_index[:, None] + order_index[None, :]).astype(jnp.float32)
    radial = jnp.exp(degree_grid[:, None, None, :] * jnp.log(shell_ratio)[None, None, :, None])
    summed = lax.optimization_barrier(jnp.sum(radial * shell_terms, axis=2))
    clipped = jnp.minimum(order_list, DEG - 1).astype(jnp.int32)
    padded = jnp.concatenate([precision, jnp.zeros_like(precision)])
    weights = jax.vmap(lambda first_degree: lax.dynamic_slice_in_dim(padded, first_degree, DEG))(order_list.astype(jnp.int32))[:, None, :]
    slot_residual = weights * (summed[clipped] - observed)
    residual = jnp.zeros((DEG, 2, DEG), jnp.float32).at[clipped].add(slot_residual)
    weighted = radial * residual[:, :, None, :]

    def adjoint_group(group_item):
        return synthesise(group_item[1], legendre_table(group_item[0], NLAT, DEG))
    adjoint = lax.map(adjoint_group, (groups, weighted.reshape(DEG // 64, 64, 2, SHELLS, DEG))).reshape(DEG, 2, SHELLS, NLAT)
    adjoint_t = jnp.transpose(adjoint, (1, 2, 3, 0))
    synth_scale = jnp.where(order_index == 0, NLON * math.sqrt(1.0 / NLON), 0.5 * NLON * math.sqrt(2.0 / NLON)).astype(jnp.float32)
    imag_keep = (order_index > 0).astype(jnp.float32)
    coefficients = adjoint_t[0] * synth_scale + 1j * (adjoint_t[1] * synth_scale * imag_keep)
    coefficients = jnp.pad(coefficients, ((0, 0), (0, 0), (0, NLON // 2 + 1 - DEG)))
    return jnp.fft.irfft(coefficients, n=NLON, axis=2)

def reference(density, momentum, observed, order_list, shell_ratio, precision):
    first_grad = likelihood(density, observed, order_list, shell_ratio, precision)
    half_momentum = momentum - 0.5 * STEP * (density + first_grad)
    new_density = density + STEP * half_momentum
    second_grad = likelihood(new_density, observed, order_list, shell_ratio, precision)
    new_momentum = half_momentum - 0.5 * STEP * (new_density + second_grad)
    return (new_density, new_momentum)
```

```python
import functools

import jax
import jax.numpy as jnp
import ml_dtypes
import numpy as np
from jax import lax
from jax.experimental import pallas as pl
from jax.experimental.pallas import tpu as pltpu
from jax.sharding import PartitionSpec as P

STEP = 0.5
LANES = 128
GROUP = 8
RENORM = 16
MESH = pl.DeviceIdType.MESH
VMEM_LIMIT = 58 * 1024 * 1024


def dot_ab(a, b):
    return lax.dot_general(a, b, (((1,), (0,)), ((), ())), preferred_element_type=jnp.float32)


def dot_abt(a, b):
    return lax.dot_general(a, b, (((1,), (1,)), ((), ())), preferred_element_type=jnp.float32)


def dot_atb(a, b):
    return lax.dot_general(a, b, (((0,), (0,)), ((), ())), preferred_element_type=jnp.float32)


def split_parts(x):
    top = x.astype(jnp.bfloat16)
    return top, (x - top.astype(jnp.float32)).astype(jnp.bfloat16)


def round_up(x, to):
    return -(-x // to) * to


class Plan:
    def __init__(self, n_shell, n_band, local_shells, lat_rows, lon_cells, degrees):
        self.n_shell, self.n_band, self.local_shells = n_shell, n_band, local_shells
        self.lat_rows, self.lon_cells, self.degrees = lat_rows, lon_cells, degrees
        self.devices = n_shell * n_band
        self.shells = n_shell * local_shells
        self.lat_total = n_band * lat_rows
        self.cells = local_shells * lat_rows
        self.own = -(-degrees // self.devices)
        self.groups = -(-self.own // GROUP)
        self.wide = 2 * self.cells
        self.tiles = -(-2 * self.wide // LANES)
        self.span = [
            (p * self.wide // LANES, -(-(p + 1) * self.wide // LANES)) for p in range(2)
        ]
        self.packed, self.row_at, rows = [], [], 0
        for g in range(self.groups):
            packed = self.own - g * GROUP <= GROUP // 2
            self.packed.append(packed)
            self.row_at.append(rows)
            used = self.tiles * (GROUP // 2 if packed else GROUP)
            if g == self.groups - 1:
                self.ratio_row = rows + used
                used += local_shells
            rows += round_up(used, 8)
        self.rows = rows
        self.depth = [
            min(degrees, round_up(degrees - g * GROUP * self.devices, 2 * RENORM))
            for g in range(self.groups)
        ]
        self.half_at = [sum(self.depth[:g]) // 2 for g in range(self.groups)]
        self.half_all = sum(self.depth) // 2
        pairs = n_band // 2
        self.per_block = max(q for q in range(1, pairs + 1) if pairs % q == 0 and q * lat_rows <= LANES)
        self.blocks = pairs // self.per_block
        self.lat_lanes = self.blocks * LANES
        self.columns = 2 * GROUP * self.shells

    def slot_of(self, g, i):
        return g * GROUP + (i % (GROUP // 2) if self.packed[g] else i)

    def fourier(self):
        n = np.arange(self.lon_cells)
        out = np.zeros((self.groups, 2, self.devices, GROUP, self.lon_cells), np.float32)
        for g in range(self.groups):
            for i in range(GROUP):
                slot = self.slot_of(g, i)
                if slot >= self.own:
                    continue
                order = slot * self.devices + np.arange(self.devices)
                live = order < self.degrees
                phase = (order[:, None] * n[None, :]) % self.lon_cells * (2.0 * np.pi / self.lon_cells)
                factor = np.where(order == 0, 1.0, np.sqrt(2.0)) * live / np.sqrt(self.lon_cells)
                out[g, 0, :, i] = factor[:, None] * np.cos(phase)
                out[g, 1, :, i] = -factor[:, None] * np.sin(phase)
        out = out.reshape(self.groups, 2, self.devices * GROUP, self.lon_cells)
        top = out.astype(ml_dtypes.bfloat16)
        low = (out - top.astype(np.float32)).astype(ml_dtypes.bfloat16)
        return top, low

    def turn(self):
        at = np.arange(self.wide)
        back = at // self.lat_rows * self.lat_rows + (self.lat_rows - 1 - at % self.lat_rows)
        return np.stack([at[:, None] == at[None, :], at[:, None] == back[None, :]])

    def placement(self):
        turn = self.turn()
        width = max(b - a for a, b in self.span) * LANES
        out = np.zeros((2, 2, width, self.wide), bool)
        for p in range(2):
            start = p * self.wide - self.span[p][0] * LANES
            out[:, p, start : start + self.wide] = turn
        return out.astype(ml_dtypes.bfloat16)

    def latitudes(self):
        lane = np.arange(self.lat_lanes)
        inside = lane % LANES
        live = inside < self.per_block * self.lat_rows
        row = lane // LANES * (self.per_block * self.lat_rows) + np.where(live, inside, 0)
        angle = (row.astype(np.float32) + np.float32(0.5)) * np.float32(np.pi / self.lat_total)
        angle = angle.astype(np.float32).astype(np.float64)
        sine = np.sin(angle).astype(np.float32)
        quadrature = np.sqrt(sine * np.float32(np.pi / self.lat_total)) * live
        rows = np.zeros((8, self.lat_lanes), np.float32)
        rows[0] = np.cos(angle)
        rows[1] = np.log(sine.astype(np.float64))
        rows[2] = quadrature
        return rows


def spectra_kernel(plan, density_ref, momentum_ref, place_ref, top_ref, low_ref, ratio_ref, out_ref,
                   field_top, field_low):
    g = pl.program_id(1)
    south = (lax.axis_index("band") >= plan.n_band // 2).astype(jnp.int32)

    @pl.when((pl.program_id(0) == 0) & (g == 0))
    def _():
        density = density_ref[...]
        ahead = (1.0 - 0.5 * STEP * STEP) * density + STEP * momentum_ref[...]
        top, low = split_parts(jnp.concatenate([density, ahead], axis=0))
        for p in range(2):
            place = place_ref[south, p]
            field_top[p] = dot_ab(place, top).astype(jnp.bfloat16)
            field_low[p] = dot_ab(place, low).astype(jnp.bfloat16)

    parts = []
    for p in range(2):
        table_top, table_low = top_ref[0, p], low_ref[0, p]
        parts.append(
            dot_abt(table_top, field_top[p]) + dot_abt(table_top, field_low[p])
            + dot_abt(table_low, field_top[p])
        )
    tiles = []
    for t in range(plan.tiles):
        tile = None
        for p, (first, last) in enumerate(plan.span):
            if first <= t < last:
                piece = parts[p][:, (t - first) * LANES : (t - first + 1) * LANES]
                tile = piece if tile is None else tile + piece
        tiles.append(tile.reshape(-1, GROUP, LANES))
    sub = lax.broadcasted_iota(jnp.int32, tiles[0].shape, 1)
    for group in range(plan.groups):
        @pl.when(g == group)
        def _(group=group):
            row = plan.row_at[group]
            if not plan.packed[group]:
                for t in range(plan.tiles):
                    out_ref[:, row + t * GROUP : row + (t + 1) * GROUP, :] = tiles[t]
                last = plan.tiles * GROUP
            else:
                half = GROUP // 2
                for t in range(0, plan.tiles - 1, 2):
                    out_ref[:, row + t * half : row + t * half + GROUP, :] = jnp.where(
                        sub < half, tiles[t], tiles[t + 1]
                    )
                if plan.tiles % 2:
                    t = plan.tiles - 1
                    out_ref[:, row + t * half : row + (t + 1) * half, :] = tiles[t][:, :half]
            if group == plan.groups - 1:
                for s in range(plan.local_shells):
                    at = plan.ratio_row + s
                    out_ref[:, at : at + 1, :] = jnp.broadcast_to(
                        ratio_ref[s : s + 1, :][None], (out_ref.shape[0], 1, LANES)
                    )


def spectra(plan, density, momentum, ratio, table):
    tall = min(plan.devices, 32)
    placement = jnp.asarray(plan.placement())
    width = placement.shape[2]
    whole = lambda shape: pl.BlockSpec(shape, lambda i, g: (0,) * len(shape))
    at_table = pl.BlockSpec((1, 2, tall * GROUP, plan.lon_cells), lambda i, g: (g, 0, i, 0))
    return pl.pallas_call(
        functools.partial(spectra_kernel, plan),
        grid=(plan.devices // tall, plan.groups),
        in_specs=[whole(density.shape), whole(momentum.shape), whole(placement.shape), at_table,
                  at_table, whole(ratio.shape)],
        out_specs=pl.BlockSpec((tall, plan.rows, LANES), lambda i, g: (i, 0, 0)),
        out_shape=jax.ShapeDtypeStruct((plan.devices, plan.rows, LANES), jnp.float32),
        scratch_shapes=[pltpu.VMEM((2, width, plan.lon_cells), jnp.bfloat16)] * 2,
        compiler_params=pltpu.CompilerParams(vmem_limit_bytes=VMEM_LIMIT),
        name="spectra",
    )(density, momentum, placement, table[0], table[1], ratio)


def exchange_kernel(plan, send_ref, recv_ref, send_sem, recv_sem):
    n, n_band = plan.devices, plan.n_band
    me = lax.axis_index("shell") * n_band + lax.axis_index("band")
    barrier = pltpu.get_barrier_semaphore()

    def peer(i):
        to = lax.rem(me + i, n)
        return to, (to // n_band, lax.rem(to, n_band))

    def greet(i, carry):
        pl.semaphore_signal(barrier, inc=1, device_id=peer(i)[1], device_id_type=MESH)
        return carry

    lax.fori_loop(1, n, greet, 0)
    pl.semaphore_wait(barrier, n - 1)
    pltpu.make_async_copy(send_ref.at[me], recv_ref.at[me], recv_sem).start()

    def send(i, carry):
        to, device = peer(i)
        pltpu.make_async_remote_copy(
            src_ref=send_ref.at[to], dst_ref=recv_ref.at[me], send_sem=send_sem, recv_sem=recv_sem,
            device_id=device, device_id_type=MESH,
        ).start()
        return carry

    lax.fori_loop(1, n, send, 0)
    pltpu.make_async_copy(recv_ref, recv_ref, recv_sem).wait()
    others = send_ref.at[pl.ds(0, n - 1)]
    pltpu.make_async_copy(others, others, send_sem).wait()


def exchange(plan, sent, collective_id):
    return pl.pallas_call(
        functools.partial(exchange_kernel, plan),
        out_shape=jax.ShapeDtypeStruct(sent.shape, sent.dtype),
        in_specs=[pl.BlockSpec(memory_space=pltpu.VMEM)],
        out_specs=pl.BlockSpec(memory_space=pltpu.VMEM),
        scratch_shapes=[pltpu.SemaphoreType.DMA, pltpu.SemaphoreType.DMA],
        compiler_params=pltpu.CompilerParams(
            collective_id=collective_id, has_side_effects=True, vmem_limit_bytes=VMEM_LIMIT
        ),
        name="exchange%d" % collective_id,
    )(sent)


def legendre(plan, group, me, seed_ref, lat_ref, table_top, table_low):
    shape = (GROUP, LANES)
    slot = lax.broadcasted_iota(jnp.int32, shape, 0) + group * GROUP
    lane = lax.broadcasted_iota(jnp.int32, shape, 1)
    order = slot * plan.devices + me
    live = (slot < plan.own) & (order < plan.degrees)
    order = jnp.where(live, order, plan.degrees)
    order_value = order.astype(jnp.float32)
    depth = plan.depth[group]
    growths, dampings = [], []
    for t in range(-(-depth // LANES)):
        step_int = lane + (t * LANES + 1)
        step = step_int.astype(jnp.float32)
        total = order_value + step
        growth = jnp.sqrt((4.0 * total * total - 1.0) / (step * (2.0 * order_value + step)))
        growths.append(jnp.where(order + step_int < plan.degrees, growth, 0.0))
        lower = (total - 1.0) * (total - 1.0)
        dampings.append(jnp.sqrt(
            (step - 1.0) * (2.0 * order_value + step - 1.0) / jnp.maximum(4.0 * lower - 1.0, 1.0)
        ))
    full = (GROUP, plan.lat_lanes)
    cosine = jnp.broadcast_to(lat_ref[0:1, :], full)
    quadrature = jnp.broadcast_to(lat_ref[2:3, :], full)
    seed = seed_ref[group * GROUP : (group + 1) * GROUP, :]
    log_value = seed[:, 1:2] * lat_ref[1:2, :] + seed[:, 0:1]
    current = jnp.where(seed[:, 1:2] < plan.degrees, jnp.ones(full, jnp.float32), 0.0)
    previous = jnp.zeros(full, jnp.float32)
    per_tile = LANES // RENORM

    for t in range(-(-depth // LANES)):
        count = min(per_tile, (depth - t * LANES) // RENORM)
        half_start = plan.half_at[group] * GROUP

        def one_span(i, carry, t=t):
            current, previous, log_value = carry
            factor = jnp.exp(log_value) * quadrature
            shift = lax.rem(LANES - i * RENORM, LANES)
            growth_tile = pltpu.roll(growths[t], shift, 1)
            damping_tile = pltpu.roll(dampings[t], shift, 1)
            values = [[], []]
            for step in range(RENORM):
                values[step % 2].append(current * factor)
                growth = growth_tile[:, step : step + 1]
                damping = damping_tile[:, step : step + 1]
                current, previous = growth * (cosine * current - damping * previous), current
            largest = jnp.maximum(jnp.abs(current), jnp.abs(previous))
            largest = jnp.where(largest == 0.0, 1.0, largest)
            row = half_start + (t * per_tile + i) * (RENORM // 2 * GROUP)
            row = pl.multiple_of(row, RENORM // 2 * GROUP)
            for parity in range(2):
                top, low = split_parts(jnp.concatenate(values[parity], axis=0))
                table_top[parity, pl.ds(row, RENORM // 2 * GROUP), :] = top
                table_low[parity, pl.ds(row, RENORM // 2 * GROUP), :] = low
            return current / largest, previous / largest, log_value + jnp.log(largest)

        current, previous, log_value = lax.fori_loop(0, count, one_span, (current, previous, log_value))


def moved(tiles, start, width, dest):
    first, offset = start // LANES, start % LANES
    shift = (dest - offset) % LANES
    turn = lambda x: pltpu.roll(x, shift, 1) if shift else x
    value = turn(tiles[first])
    if offset + width > LANES:
        lane = lax.broadcasted_iota(jnp.int32, value.shape, 1)
        value = jnp.where(lane < dest + LANES - offset, value, turn(tiles[first + 1]))
    return value


def gather_fields(plan, group, recv_ref, fold_top, fold_low):
    row, half = plan.row_at[group], GROUP // 2

    def tiles_of(device):
        out = []
        for t in range(plan.tiles):
            if not plan.packed[group]:
                out.append(recv_ref[device, row + t * GROUP : row + (t + 1) * GROUP, :])
            else:
                at = row + t // 2 * GROUP
                pair = recv_ref[device, at : at + GROUP, :]
                out.append(pltpu.roll(pair, half, 0) if t % 2 else pair)
        return out

    lane = lax.broadcasted_iota(jnp.int32, (GROUP, LANES), 1)
    width = plan.lat_rows
    for sy in range(plan.n_shell):
        for block in range(plan.blocks):
            sides = {}
            for inside in range(plan.per_block):
                band = block * plan.per_block + inside
                for side, source in enumerate((band, plan.n_band - 1 - band)):
                    tiles = tiles_of(sy * plan.n_band + source)
                    for piece in range(4 * plan.local_shells):
                        value = moved(tiles, piece * width, width, inside * width)
                        if inside:
                            value = jnp.where(lane < inside * width, sides[side, piece], value)
                        sides[side, piece] = value
            for field in range(2):
                for s in range(plan.local_shells):
                    pieces = [(p * 2 + field) * plan.local_shells + s for p in range(2)]
                    north = jnp.concatenate([sides[0, at] for at in pieces], axis=0)
                    south = jnp.concatenate([sides[1, at] for at in pieces], axis=0)
                    start = field * plan.columns + (sy * plan.local_shells + s) * 2 * GROUP
                    for parity, folded in enumerate((north + south, north - south)):
                        top, low = split_parts(folded)
                        at = (parity, pl.ds(start, 2 * GROUP), pl.ds(block * LANES, LANES))
                        fold_top[at] = top
                        fold_low[at] = low


def scatter_fields(plan, group, grids, send_ref):
    row, half, width = plan.row_at[group], GROUP // 2, plan.lat_rows
    lane = lax.broadcasted_iota(jnp.int32, (GROUP, LANES), 1)
    sub = lax.broadcasted_iota(jnp.int32, (GROUP, LANES), 0)
    for sy in range(plan.n_shell):
        for band in range(plan.n_band):
            side = int(band >= plan.n_band // 2)
            mirrored = plan.n_band - 1 - band if side else band
            block, inside = mirrored // plan.per_block, mirrored % plan.per_block
            tiles = []
            for t in range(plan.tiles):
                tile = None
                for piece in range(4 * plan.local_shells):
                    start = piece * width - t * LANES
                    if start + width <= 0 or start >= LANES:
                        continue
                    p, field, s = piece // (2 * plan.local_shells), piece // plan.local_shells % 2, piece % plan.local_shells
                    at = ((sy * plan.local_shells + s) * 2 + p) * GROUP
                    value = grids[field][side][at : at + GROUP, pl.ds(block * LANES, LANES)]
                    shift = (start - inside * width) % LANES
                    if shift:
                        value = pltpu.roll(value, shift, 1)
                    tile = value if tile is None else jnp.where(lane < start, tile, value)
                tiles.append(tile)
            device = sy * plan.n_band + band
            if not plan.packed[group]:
                for t in range(plan.tiles):
                    send_ref[device, row + t * GROUP : row + (t + 1) * GROUP, :] = tiles[t]
            else:
                for t in range(0, plan.tiles, 2):
                    pair = tiles[t]
                    if t + 1 < plan.tiles:
                        pair = jnp.where(sub < half, pair, pltpu.roll(tiles[t + 1], half, 0))
                    send_ref[device, row + t * half : row + t * half + GROUP, :] = pair


def misfit_group(plan, group, me, log_ratio, recv_ref, seen_ref, weight_ref, table_top, table_low,
                 fold_top, fold_low, wanted_ref, grid_ref, send_ref):
    columns = plan.columns
    gather_fields(plan, group, recv_ref, fold_top, fold_low)
    half_depth = plan.depth[group] // 2
    half_at = plan.half_at[group]
    chunk = max(c for c in range(RENORM // 2, 65, RENORM // 2) if half_depth % c == 0)
    shape = (chunk, columns)
    lane = lax.broadcasted_iota(jnp.int32, shape, 1)
    order = (lax.rem(lane, GROUP) + group * GROUP) * plan.devices + me
    imaginary = lax.rem(lane // GROUP, 2) == 1
    keep = jnp.where((order == 0) & imaginary, 0.0, 1.0)
    offset = lax.broadcasted_iota(jnp.int32, shape, 0) * 2 + order
    own_row = lax.broadcasted_iota(jnp.int32, (GROUP, columns), 0)
    own_lane = lax.rem(lax.broadcasted_iota(jnp.int32, (GROUP, columns), 1), GROUP)
    own = jnp.where(own_row == own_lane, 1.0, 0.0)

    def over_shells(x):
        shift = 2 * GROUP
        while shift < columns:
            x = x + pltpu.roll(x, shift, 1)
            shift *= 2
        return x

    def rows_at(c):
        start = pl.multiple_of(half_at * GROUP + c * (chunk * GROUP), chunk * GROUP)
        return pl.ds(start, chunk * GROUP)

    def pick(values):
        return jnp.sum(values.reshape(chunk, GROUP, columns) * own[None], axis=1)

    def spread(values):
        wide = values[:, None, :] * own[None]
        return split_parts(wide.reshape(chunk * GROUP, columns))

    for parity in range(2):
        def radial_at(c, parity=parity):
            return jnp.exp((offset + (c * (2 * chunk) + parity)).astype(jnp.float32) * log_ratio)

        def adjoint(c, weighted, parity=parity):
            rows = rows_at(c)
            top, low = spread(weighted)
            return (dot_atb(top, table_top[parity, rows, :]) + dot_atb(low, table_top[parity, rows, :])
                    + dot_atb(top, table_low[parity, rows, :]))

        def first_pass(c, carry, parity=parity):
            rows = rows_at(c)
            tall = pl.ds(pl.multiple_of(half_at + c * chunk, chunk), chunk)
            top = table_top[parity, rows, :]
            terms = (dot_abt(top, fold_top[parity]) + dot_abt(top, fold_low[parity])
                     + dot_abt(table_low[parity, rows, :], fold_top[parity]))
            radial = radial_at(c)
            seen = seen_ref[parity, tall, :]
            first = over_shells(pick(terms[:, :columns]) * radial - seen)
            ahead = over_shells(pick(terms[:, columns:]) * radial - seen)
            wanted_ref[pl.ds(pl.multiple_of(c * chunk, chunk), chunk), :] = ahead
            grid_ref[0, parity] += adjoint(c, radial * weight_ref[parity, tall, :] * first)
            return carry

        grid_ref[0, parity] = jnp.zeros_like(grid_ref[0, parity])
        lax.fori_loop(0, half_depth // chunk, first_pass, 0)
        again_top, again_low = split_parts(2.0 * grid_ref[0, parity])
        fold_top[parity, 0:columns, :] = again_top
        fold_low[parity, 0:columns, :] = again_low

        def second_pass(c, carry, parity=parity):
            rows = rows_at(c)
            tall = pl.ds(pl.multiple_of(half_at + c * chunk, chunk), chunk)
            top = table_top[parity, rows, :]
            folded_top, folded_low = fold_top[parity, 0:columns, :], fold_low[parity, 0:columns, :]
            terms = (dot_abt(top, folded_top) + dot_abt(top, folded_low)
                     + dot_abt(table_low[parity, rows, :], folded_top))
            radial = radial_at(c)
            back = over_shells(pick(terms) * radial) * keep
            ahead = wanted_ref[pl.ds(pl.multiple_of(c * chunk, chunk), chunk), :]
            misfit = ahead - (0.5 * STEP * STEP) * back
            grid_ref[1, parity] += adjoint(c, radial * weight_ref[parity, tall, :] * misfit)
            return carry

        grid_ref[1, parity] = jnp.zeros_like(grid_ref[1, parity])
        lax.fori_loop(0, half_depth // chunk, second_pass, 0)

    for field in range(2):
        even, odd = grid_ref[field, 0], grid_ref[field, 1]
        grid_ref[field, 0] = even + odd
        grid_ref[field, 1] = even - odd
    grids = [[grid_ref.at[field, side] for side in range(2)] for field in range(2)]
    scatter_fields(plan, group, grids, send_ref)


def misfit_kernel(plan, recv_ref, seen_ref, weight_ref, seed_ref, lat_ref, send_ref, table_top,
                  table_low, fold_top, fold_low, wanted_ref, grid_ref):
    me = lax.axis_index("shell") * plan.n_band + lax.axis_index("band")
    for group in range(plan.groups):
        legendre(plan, group, me, seed_ref, lat_ref, table_top, table_low)
    lane = lax.broadcasted_iota(jnp.int32, (1, plan.columns), 1)
    ratio = jnp.ones((1, plan.columns), jnp.float32)
    for sy in range(plan.n_shell):
        for s in range(plan.local_shells):
            at = plan.ratio_row + s
            value = recv_ref[sy * plan.n_band, at : at + 1, :]
            ratio = jnp.where(lane // (2 * GROUP) == sy * plan.local_shells + s, value, ratio)
    log_ratio = jnp.log(ratio)
    for group in range(plan.groups):
        misfit_group(plan, group, me, log_ratio, recv_ref, seen_ref, weight_ref, table_top, table_low,
                     fold_top, fold_low, wanted_ref, grid_ref, send_ref)


def misfit(plan, received, seen, weight, seed, lat):
    vmem = pl.BlockSpec(memory_space=pltpu.VMEM)
    table = pltpu.VMEM((2, plan.half_all * GROUP, plan.lat_lanes), jnp.bfloat16)
    fold = pltpu.VMEM((2, 2 * plan.columns, plan.lat_lanes), jnp.bfloat16)
    return pl.pallas_call(
        functools.partial(misfit_kernel, plan),
        out_shape=jax.ShapeDtypeStruct(received.shape, received.dtype),
        in_specs=[vmem] * 5,
        out_specs=vmem,
        scratch_shapes=[table, table, fold, fold,
                        pltpu.VMEM((plan.depth[0] // 2, plan.columns), jnp.float32),
                        pltpu.VMEM((2, 2, plan.columns, plan.lat_lanes), jnp.float32)],
        compiler_params=pltpu.CompilerParams(vmem_limit_bytes=VMEM_LIMIT),
        name="misfit",
    )(received, seen, weight, seed, lat)


def grids_kernel(plan, recv_ref, top_ref, low_ref, turn_ref, density_ref, momentum_ref, new_density_ref,
                 new_momentum_ref, total):
    step, g = pl.program_id(0), pl.program_id(1)
    south = (lax.axis_index("band") >= plan.n_band // 2).astype(jnp.int32)

    @pl.when((step == 0) & (g == 0))
    def _():
        total[...] = jnp.zeros_like(total)

    half = GROUP // 2
    for group in range(plan.groups):
        @pl.when(g == group)
        def _(group=group):
            row = plan.row_at[group]
            tiles = []
            for t in range(plan.tiles):
                if not plan.packed[group]:
                    tile = recv_ref[:, row + t * GROUP : row + (t + 1) * GROUP, :]
                else:
                    at = row + t // 2 * GROUP
                    tile = recv_ref[:, at : at + GROUP, :]
                    sub = lax.broadcasted_iota(jnp.int32, tile.shape, 1)
                    tile = jnp.where((sub < half) == (t % 2 == 0), tile, 0.0)
                tiles.append(tile.reshape(-1, LANES))
            for p, (first, last) in enumerate(plan.span):
                top, low = split_parts(jnp.concatenate(tiles[first:last], axis=1))
                table_top, table_low = top_ref[0, p], low_ref[0, p]
                total[p, 0 : (last - first) * LANES] += (
                    dot_atb(top, table_top) + dot_atb(low, table_top) + dot_atb(top, table_low)
                )

    @pl.when((step == pl.num_programs(0) - 1) & (g == plan.groups - 1))
    def _():
        grid = jnp.zeros((plan.wide, plan.lon_cells), jnp.float32)
        for p, (first, last) in enumerate(plan.span):
            start = p * plan.wide - first * LANES
            grid = grid + total[p, start : start + plan.wide]
        top, low = split_parts(grid)
        turn = turn_ref[south]
        grid = dot_ab(turn, top) + dot_ab(turn, low)
        density, momentum = density_ref[...], momentum_ref[...]
        half_momentum = momentum - 0.5 * STEP * (density + grid[: plan.cells])
        new_density = density + STEP * half_momentum
        new_density_ref[...] = new_density
        new_momentum_ref[...] = half_momentum - 0.5 * STEP * (new_density + grid[plan.cells :])


def grids(plan, returned, table, density, momentum):
    tall = min(plan.devices, 32)
    turn = jnp.asarray(plan.turn().astype(ml_dtypes.bfloat16))
    width = max(b - a for a, b in plan.span) * LANES
    whole = lambda shape: pl.BlockSpec(shape, lambda i, g: (0,) * len(shape))
    at_table = pl.BlockSpec((1, 2, tall * GROUP, plan.lon_cells), lambda i, g: (g, 0, i, 0))
    shape = jax.ShapeDtypeStruct(density.shape, jnp.float32)
    return pl.pallas_call(
        functools.partial(grids_kernel, plan),
        grid=(plan.devices // tall, plan.groups),
        in_specs=[pl.BlockSpec((tall, plan.rows, LANES), lambda i, g: (i, 0, 0)), at_table, at_table,
                  whole(turn.shape), whole(density.shape), whole(momentum.shape)],
        out_specs=[whole(density.shape)] * 2,
        out_shape=[shape, shape],
        scratch_shapes=[pltpu.VMEM((2, width, plan.lon_cells), jnp.float32)],
        compiler_params=pltpu.CompilerParams(vmem_limit_bytes=VMEM_LIMIT),
        name="grids",
    )(returned, table[0], table[1], turn, density, momentum)


def by_degree(plan, values):
    slots = plan.groups * GROUP
    values = jnp.pad(values, ((0, slots - values.shape[0]), (0, 0), (0, 0)))
    parts = []
    for g in range(plan.groups):
        part = values[g * GROUP : (g + 1) * GROUP, :, : plan.depth[g]]
        part = part.reshape(GROUP, values.shape[1], plan.depth[g] // 2, 2)
        parts.append(part.transpose(3, 2, 1, 0))
    return jnp.concatenate(parts, axis=1)


def body(density, momentum, observed, order_list, shell_ratio, precision):
    slots, _, degrees = observed.shape
    local_shells, lat_rows, lon_cells = density.shape
    n_shell, n_band = lax.axis_size("shell"), lax.axis_size("band")
    plan = Plan(n_shell, n_band, local_shells, lat_rows, lon_cells, degrees)
    row, band = lax.axis_index("shell"), lax.axis_index("band")
    me = row * n_band + band

    local_orders = lax.dynamic_slice_in_dim(order_list, band * slots, slots)
    slot = jnp.arange(plan.own, dtype=jnp.int32)
    wanted = slot[None, :] * plan.devices + row * n_band + jnp.arange(n_band, dtype=jnp.int32)[:, None]
    wanted = jnp.where(wanted < degrees, wanted, -1).reshape(-1)
    chosen = (wanted[:, None] == local_orders[None, :]).astype(jnp.float32)
    routed = jnp.einsum("qt,tk->qk", chosen, observed.reshape(slots, 2 * degrees),
                        precision=lax.Precision.HIGH, preferred_element_type=jnp.float32)
    own_seen = lax.psum_scatter(routed, "band", scatter_dimension=0, tiled=True)
    seen = by_degree(plan, own_seen.reshape(plan.own, 2, degrees))
    seen = seen.reshape(2, plan.half_all, 2 * GROUP)
    seen = jnp.pad(seen, ((0, 0), (0, 0), (0, plan.columns - 2 * GROUP)))

    orders = jnp.arange(plan.groups * GROUP, dtype=jnp.int32)
    orders = jnp.where(orders < plan.own, orders * plan.devices + me, degrees)
    orders = jnp.minimum(orders, degrees)
    padded = jnp.pad(precision, (0, plan.own * plan.devices + degrees))
    weight = jnp.stack([
        lax.dynamic_slice_in_dim(padded, i * plan.devices + me, degrees) for i in range(plan.own)
    ])
    weight = by_degree(plan, weight[:, None, :]).reshape(2, plan.half_all, GROUP)
    weight = jnp.tile(weight, (1, 1, plan.columns // GROUP))
    order_value = orders.astype(jnp.float32)
    seed = 0.5 * (
        jnp.log(order_value + 0.5)
        + lax.lgamma(2.0 * order_value + 1.0)
        - order_value * jnp.log(4.0)
        - 2.0 * lax.lgamma(order_value + 1.0)
    )
    seed = jnp.stack([seed, order_value], axis=1)

    table = [jnp.asarray(x) for x in plan.fourier()]
    lat = jnp.asarray(plan.latitudes())
    ratio = jnp.broadcast_to(shell_ratio[:, None], (local_shells, LANES))
    flat_density = density.reshape(plan.cells, lon_cells)
    flat_momentum = momentum.reshape(plan.cells, lon_cells)
    sent = spectra(plan, flat_density, flat_momentum, ratio, table)
    received = exchange(plan, sent, 0)
    result = misfit(plan, received, seen, weight, seed, lat)
    returned = exchange(plan, result, 1)
    new_density, new_momentum = grids(plan, returned, table, flat_density, flat_momentum)
    return new_density.reshape(density.shape), new_momentum.reshape(density.shape)


def solution(mesh):
    in_specs = (
        P("shell", "band", None),
        P("shell", "band", None),
        P("band", None, None),
        P(),
        P("shell"),
        P(),
    )
    out_specs = (P("shell", "band", None), P("shell", "band", None))
    return jax.shard_map(body, mesh=mesh, in_specs=in_specs, out_specs=out_specs, check_vma=False)
```

```python
import functools

import jax
import jax.numpy as jnp
import ml_dtypes
import numpy as np
from jax import lax
from jax.experimental import pallas as pl
from jax.experimental.pallas import tpu as pltpu
from jax.sharding import PartitionSpec as P

STEP = 0.5
LANES = 128
GROUP = 8
RENORM = 16
MESH = pl.DeviceIdType.MESH
VMEM_LIMIT = 58 * 1024 * 1024


def dot_ab(a, b):
    return lax.dot_general(a, b, (((1,), (0,)), ((), ())), preferred_element_type=jnp.float32)


def dot_abt(a, b):
    return lax.dot_general(a, b, (((1,), (1,)), ((), ())), preferred_element_type=jnp.float32)


def dot_atb(a, b):
    return lax.dot_general(a, b, (((0,), (0,)), ((), ())), preferred_element_type=jnp.float32)


def split_parts(x):
    top = x.astype(jnp.bfloat16)
    return top, (x - top.astype(jnp.float32)).astype(jnp.bfloat16)


def round_up(x, to):
    return -(-x // to) * to


class Plan:
    def __init__(self, n_shell, n_band, local_shells, lat_rows, lon_cells, degrees):
        self.n_shell, self.n_band, self.local_shells = n_shell, n_band, local_shells
        self.lat_rows, self.lon_cells, self.degrees = lat_rows, lon_cells, degrees
        self.devices = n_shell * n_band
        self.shells = n_shell * local_shells
        self.lat_total = n_band * lat_rows
        self.cells = local_shells * lat_rows
        self.own = -(-degrees // self.devices)
        self.groups = -(-self.own // GROUP)
        self.wide = 2 * self.cells
        self.tiles = -(-2 * self.wide // LANES)
        self.span = [
            (p * self.wide // LANES, -(-(p + 1) * self.wide // LANES)) for p in range(2)
        ]
        self.turns = [self.groups - 1] + list(range(self.groups - 1))
        self.packed, self.row_at, rows = [], [], 0
        for g in range(self.groups):
            packed = self.own - g * GROUP <= GROUP // 2
            self.packed.append(packed)
            self.row_at.append(rows)
            used = self.tiles * (GROUP // 2 if packed else GROUP)
            if g == self.groups - 1:
                self.ratio_row = rows + used
                used += local_shells
            rows += round_up(used, 8)
        self.rows = rows
        self.depth = [
            min(degrees, round_up(degrees - g * GROUP * self.devices, 2 * RENORM))
            for g in range(self.groups)
        ]
        self.half_at = [sum(self.depth[:g]) // 2 for g in range(self.groups)]
        self.half_all = sum(self.depth) // 2
        pairs = n_band // 2
        self.per_block = max(q for q in range(1, pairs + 1) if pairs % q == 0 and q * lat_rows <= LANES)
        self.blocks = pairs // self.per_block
        self.lat_lanes = self.blocks * LANES
        self.columns = 2 * GROUP * self.shells
        self.degree_tiles = [round_up(depth, LANES) // LANES for depth in self.depth]
        self.degree_at = [sum(self.degree_tiles[:g]) * LANES for g in range(self.groups)]
        self.degree_all = sum(self.degree_tiles) * LANES
        self.seen_at = [2 * GROUP * sum(self.degree_tiles[:g]) for g in range(self.groups)]
        self.seen_rows = 2 * GROUP * sum(self.degree_tiles)

    def slot_of(self, g, i):
        return g * GROUP + (i % (GROUP // 2) if self.packed[g] else i)

    def fourier(self):
        n = np.arange(self.lon_cells)
        out = np.zeros((self.groups, 2, self.devices, GROUP, self.lon_cells), np.float32)
        for g in range(self.groups):
            for i in range(GROUP):
                slot = self.slot_of(g, i)
                if slot >= self.own:
                    continue
                order = slot * self.devices + np.arange(self.devices)
                live = order < self.degrees
                phase = (order[:, None] * n[None, :]) % self.lon_cells * (2.0 * np.pi / self.lon_cells)
                factor = np.where(order == 0, 1.0, np.sqrt(2.0)) * live / np.sqrt(self.lon_cells)
                out[g, 0, :, i] = factor[:, None] * np.cos(phase)
                out[g, 1, :, i] = -factor[:, None] * np.sin(phase)
        out = out.reshape(self.groups, 2, self.devices * GROUP, self.lon_cells)
        top = out.astype(ml_dtypes.bfloat16)
        low = (out - top.astype(np.float32)).astype(ml_dtypes.bfloat16)
        return top, low

    def turn(self):
        at = np.arange(self.wide)
        back = at // self.lat_rows * self.lat_rows + (self.lat_rows - 1 - at % self.lat_rows)
        return np.stack([at[:, None] == at[None, :], at[:, None] == back[None, :]])

    def placement(self):
        turn = self.turn()
        width = max(b - a for a, b in self.span) * LANES
        out = np.zeros((2, 2, width, self.wide), bool)
        for p in range(2):
            start = p * self.wide - self.span[p][0] * LANES
            out[:, p, start : start + self.wide] = turn
        return out.astype(ml_dtypes.bfloat16)

    def latitudes(self):
        lane = np.arange(self.lat_lanes)
        inside = lane % LANES
        live = inside < self.per_block * self.lat_rows
        row = lane // LANES * (self.per_block * self.lat_rows) + np.where(live, inside, 0)
        angle = (row.astype(np.float32) + np.float32(0.5)) * np.float32(np.pi / self.lat_total)
        angle = angle.astype(np.float32).astype(np.float64)
        sine = np.sin(angle).astype(np.float32)
        quadrature = np.sqrt(sine * np.float32(np.pi / self.lat_total)) * live
        rows = np.zeros((8, self.lat_lanes), np.float32)
        rows[0] = np.cos(angle)
        rows[1] = np.log(sine.astype(np.float64))
        rows[2] = quadrature
        return rows


def route_observed(plan, orders_ref, observed_ref, routed_ref):
    slots = plan.groups * GROUP
    row, band = lax.axis_index("shell"), lax.axis_index("band")
    orders = orders_ref[pl.ds(band, 1), :]
    shape = (plan.n_band, slots, orders.shape[1])
    slot = lax.broadcasted_iota(jnp.int32, shape, 1)
    owner = lax.broadcasted_iota(jnp.int32, shape, 0) + row * plan.n_band
    wanted = slot * plan.devices + owner
    wanted = jnp.where((slot < plan.own) & (wanted < plan.degrees), wanted, -1)
    chosen = jnp.where(wanted == orders[None], 1.0, 0.0).reshape(plan.n_band * slots, -1)
    chosen = chosen.astype(jnp.bfloat16)
    for p in range(2):
        top, low = split_parts(observed_ref[:, p, :])
        rows = (dot_ab(chosen, top) + dot_ab(chosen, low)).reshape(plan.n_band, slots, plan.degrees)
        for g in range(plan.groups):
            for t in range(plan.degree_tiles[g]):
                at = plan.seen_at[g] + (p * plan.degree_tiles[g] + t) * GROUP
                routed_ref[:, at : at + GROUP, :] = rows[
                    :, g * GROUP : (g + 1) * GROUP, t * LANES : (t + 1) * LANES
                ]


def spectra_kernel(plan, density_ref, momentum_ref, place_ref, top_ref, low_ref, ratio_ref, orders_ref,
                   observed_ref, out_ref, routed_ref, field_top, field_low):
    g = pl.program_id(1)
    south = (lax.axis_index("band") >= plan.n_band // 2).astype(jnp.int32)

    @pl.when((pl.program_id(0) == 0) & (g == 0))
    def _():
        route_observed(plan, orders_ref, observed_ref, routed_ref)
        density = density_ref[...]
        ahead = (1.0 - 0.5 * STEP * STEP) * density + STEP * momentum_ref[...]
        top, low = split_parts(jnp.concatenate([density, ahead], axis=0))
        for p in range(2):
            place = place_ref[south, p]
            field_top[p] = dot_ab(place, top).astype(jnp.bfloat16)
            field_low[p] = dot_ab(place, low).astype(jnp.bfloat16)

    parts = []
    for p in range(2):
        table_top, table_low = top_ref[0, p], low_ref[0, p]
        parts.append(
            dot_abt(table_top, field_top[p]) + dot_abt(table_top, field_low[p])
            + dot_abt(table_low, field_top[p])
        )
    tiles = []
    for t in range(plan.tiles):
        tile = None
        for p, (first, last) in enumerate(plan.span):
            if first <= t < last:
                piece = parts[p][:, (t - first) * LANES : (t - first + 1) * LANES]
                tile = piece if tile is None else tile + piece
        tiles.append(tile.reshape(-1, GROUP, LANES))
    sub = lax.broadcasted_iota(jnp.int32, tiles[0].shape, 1)
    for group in range(plan.groups):
        @pl.when(g == group)
        def _(group=group):
            row = plan.row_at[group]
            if not plan.packed[group]:
                for t in range(plan.tiles):
                    out_ref[:, row + t * GROUP : row + (t + 1) * GROUP, :] = tiles[t]
                last = plan.tiles * GROUP
            else:
                half = GROUP // 2
                for t in range(0, plan.tiles - 1, 2):
                    out_ref[:, row + t * half : row + t * half + GROUP, :] = jnp.where(
                        sub < half, tiles[t], tiles[t + 1]
                    )
                if plan.tiles % 2:
                    t = plan.tiles - 1
                    out_ref[:, row + t * half : row + (t + 1) * half, :] = tiles[t][:, :half]
            if group == plan.groups - 1:
                for s in range(plan.local_shells):
                    at = plan.ratio_row + s
                    out_ref[:, at : at + 1, :] = jnp.broadcast_to(
                        ratio_ref[s : s + 1, :][None], (out_ref.shape[0], 1, LANES)
                    )


def spectra(plan, density, momentum, ratio, table, orders, observed):
    tall = min(plan.devices, 32)
    placement = jnp.asarray(plan.placement())
    width = placement.shape[2]
    whole = lambda shape: pl.BlockSpec(shape, lambda i, g: (0,) * len(shape))
    at_table = pl.BlockSpec((1, 2, tall * GROUP, plan.lon_cells), lambda i, g: (g, 0, i, 0))
    return pl.pallas_call(
        functools.partial(spectra_kernel, plan),
        grid=(plan.devices // tall, plan.groups),
        in_specs=[whole(density.shape), whole(momentum.shape), whole(placement.shape), at_table,
                  at_table, whole(ratio.shape), whole(orders.shape), whole(observed.shape)],
        out_specs=[pl.BlockSpec((tall, plan.rows, LANES), lambda i, g: (i, 0, 0)),
                   whole((plan.n_band, plan.seen_rows, LANES))],
        out_shape=[jax.ShapeDtypeStruct((plan.devices, plan.rows, LANES), jnp.float32),
                   jax.ShapeDtypeStruct((plan.n_band, plan.seen_rows, LANES), jnp.float32)],
        scratch_shapes=[pltpu.VMEM((2, width, plan.lon_cells), jnp.bfloat16)] * 2,
        compiler_params=pltpu.CompilerParams(vmem_limit_bytes=VMEM_LIMIT),
        name="spectra",
    )(density, momentum, placement, table[0], table[1], ratio, orders, observed)


def legendre(plan, group, me, seed_ref, lat_ref, table_top, table_low):
    shape = (GROUP, LANES)
    slot = lax.broadcasted_iota(jnp.int32, shape, 0) + group * GROUP
    lane = lax.broadcasted_iota(jnp.int32, shape, 1)
    order = slot * plan.devices + me
    live = (slot < plan.own) & (order < plan.degrees)
    order = jnp.where(live, order, plan.degrees)
    order_value = order.astype(jnp.float32)
    depth = plan.depth[group]
    growths, dampings = [], []
    for t in range(-(-depth // LANES)):
        step_int = lane + (t * LANES + 1)
        step = step_int.astype(jnp.float32)
        total = order_value + step
        growth = jnp.sqrt((4.0 * total * total - 1.0) / (step * (2.0 * order_value + step)))
        growths.append(jnp.where(order + step_int < plan.degrees, growth, 0.0))
        lower = (total - 1.0) * (total - 1.0)
        dampings.append(jnp.sqrt(
            (step - 1.0) * (2.0 * order_value + step - 1.0) / jnp.maximum(4.0 * lower - 1.0, 1.0)
        ))
    full = (GROUP, plan.lat_lanes)
    cosine = jnp.broadcast_to(lat_ref[0:1, :], full)
    quadrature = jnp.broadcast_to(lat_ref[2:3, :], full)
    seed = seed_ref[group * GROUP : (group + 1) * GROUP, :]
    device = lax.broadcasted_iota(jnp.int32, seed.shape, 1)
    seed = jnp.sum(jnp.where(device == me, seed, 0.0), axis=1, keepdims=True)
    orders = order_value[:, 0:1]
    log_value = orders * lat_ref[1:2, :] + seed
    current = jnp.where(orders < plan.degrees, jnp.ones(full, jnp.float32), 0.0)
    previous = jnp.zeros(full, jnp.float32)
    per_tile = LANES // RENORM

    for t in range(-(-depth // LANES)):
        count = min(per_tile, (depth - t * LANES) // RENORM)
        half_start = plan.half_at[group] * GROUP

        def one_span(i, carry, t=t):
            current, previous, log_value = carry
            factor = jnp.exp(log_value) * quadrature
            shift = lax.rem(LANES - i * RENORM, LANES)
            growth_tile = pltpu.roll(growths[t], shift, 1)
            damping_tile = pltpu.roll(dampings[t], shift, 1)
            values = [[], []]
            for step in range(RENORM):
                values[step % 2].append(current * factor)
                growth = growth_tile[:, step : step + 1]
                damping = damping_tile[:, step : step + 1]
                current, previous = growth * (cosine * current - damping * previous), current
            largest = jnp.maximum(jnp.abs(current), jnp.abs(previous))
            largest = jnp.where(largest == 0.0, 1.0, largest)
            row = half_start + (t * per_tile + i) * (RENORM // 2 * GROUP)
            row = pl.multiple_of(row, RENORM // 2 * GROUP)
            for parity in range(2):
                top, low = split_parts(jnp.concatenate(values[parity], axis=0))
                table_top[parity, pl.ds(row, RENORM // 2 * GROUP), :] = top
                table_low[parity, pl.ds(row, RENORM // 2 * GROUP), :] = low
            return current / largest, previous / largest, log_value + jnp.log(largest)

        current, previous, log_value = lax.fori_loop(0, count, one_span, (current, previous, log_value))


def moved(tiles, start, width, dest):
    first, offset = start // LANES, start % LANES
    shift = (dest - offset) % LANES
    turn = lambda x: pltpu.roll(x, shift, 1) if shift else x
    value = turn(tiles[first])
    if offset + width > LANES:
        lane = lax.broadcasted_iota(jnp.int32, value.shape, 1)
        value = jnp.where(lane < dest + LANES - offset, value, turn(tiles[first + 1]))
    return value


def gather_fields(plan, group, recv_ref, fold_top, fold_low):
    row, half = plan.row_at[group], GROUP // 2

    def tiles_of(device):
        out = []
        for t in range(plan.tiles):
            if not plan.packed[group]:
                out.append(recv_ref[device, row + t * GROUP : row + (t + 1) * GROUP, :])
            else:
                at = row + t // 2 * GROUP
                pair = recv_ref[device, at : at + GROUP, :]
                out.append(pltpu.roll(pair, half, 0) if t % 2 else pair)
        return out

    lane = lax.broadcasted_iota(jnp.int32, (GROUP, LANES), 1)
    width = plan.lat_rows
    for sy in range(plan.n_shell):
        for block in range(plan.blocks):
            sides = {}
            for inside in range(plan.per_block):
                band = block * plan.per_block + inside
                for side, source in enumerate((band, plan.n_band - 1 - band)):
                    tiles = tiles_of(sy * plan.n_band + source)
                    for piece in range(4 * plan.local_shells):
                        value = moved(tiles, piece * width, width, inside * width)
                        if inside:
                            value = jnp.where(lane < inside * width, sides[side, piece], value)
                        sides[side, piece] = value
            for field in range(2):
                for s in range(plan.local_shells):
                    pieces = [(p * 2 + field) * plan.local_shells + s for p in range(2)]
                    north = jnp.concatenate([sides[0, at] for at in pieces], axis=0)
                    south = jnp.concatenate([sides[1, at] for at in pieces], axis=0)
                    start = field * plan.columns + (sy * plan.local_shells + s) * 2 * GROUP
                    for parity, folded in enumerate((north + south, north - south)):
                        top, low = split_parts(folded)
                        at = (parity, pl.ds(start, 2 * GROUP), pl.ds(block * LANES, LANES))
                        fold_top[at] = top
                        fold_low[at] = low


def scatter_fields(plan, group, grids, send_ref):
    row, half, width = plan.row_at[group], GROUP // 2, plan.lat_rows
    lane = lax.broadcasted_iota(jnp.int32, (GROUP, LANES), 1)
    sub = lax.broadcasted_iota(jnp.int32, (GROUP, LANES), 0)
    for sy in range(plan.n_shell):
        for band in range(plan.n_band):
            side = int(band >= plan.n_band // 2)
            mirrored = plan.n_band - 1 - band if side else band
            block, inside = mirrored // plan.per_block, mirrored % plan.per_block
            tiles = []
            for t in range(plan.tiles):
                tile = None
                for piece in range(4 * plan.local_shells):
                    start = piece * width - t * LANES
                    if start + width <= 0 or start >= LANES:
                        continue
                    p, field, s = piece // (2 * plan.local_shells), piece // plan.local_shells % 2, piece % plan.local_shells
                    at = ((sy * plan.local_shells + s) * 2 + p) * GROUP
                    value = grids[field][side][at : at + GROUP, pl.ds(block * LANES, LANES)]
                    shift = (start - inside * width) % LANES
                    if shift:
                        value = pltpu.roll(value, shift, 1)
                    tile = value if tile is None else jnp.where(lane < start, tile, value)
                tiles.append(tile)
            device = sy * plan.n_band + band
            if not plan.packed[group]:
                for t in range(plan.tiles):
                    send_ref[device, row + t * GROUP : row + (t + 1) * GROUP, :] = tiles[t]
            else:
                for t in range(0, plan.tiles, 2):
                    pair = tiles[t]
                    if t + 1 < plan.tiles:
                        pair = jnp.where(sub < half, pair, pltpu.roll(tiles[t + 1], half, 0))
                    send_ref[device, row + t * half : row + t * half + GROUP, :] = pair


def degree_lanes(plan, group, me, precision_ref, total, weight_ref, seen_ref):
    shift = lax.rem(precision_ref.shape[1] - me, precision_ref.shape[1])
    precision = pltpu.roll(precision_ref[group * GROUP : (group + 1) * GROUP, :], shift, 1)
    copies = plan.columns // GROUP
    nothing = jnp.zeros((plan.columns - 2 * GROUP, LANES), jnp.float32)
    for t in range(plan.degree_tiles[group]):
        rows = pl.ds(plan.degree_at[group] + t * LANES, LANES)
        tile = precision[:, t * LANES : (t + 1) * LANES]
        weight_ref[rows, :] = jnp.concatenate([tile] * copies, axis=0).T
        tiles = []
        for p in range(2):
            at = plan.seen_at[group] + (p * plan.degree_tiles[group] + t) * GROUP
            tiles.append(total[at : at + GROUP, :])
        seen_ref[rows, :] = jnp.concatenate(tiles + [nothing], axis=0).T


def misfit_group(plan, group, me, log_ratio, recv_ref, seen_ref, weight_ref, table_top, table_low,
                 fold_top, fold_low, wanted_ref, grid_ref, send_ref):
    columns = plan.columns
    gather_fields(plan, group, recv_ref, fold_top, fold_low)
    half_depth = plan.depth[group] // 2
    half_at = plan.half_at[group]
    chunk = max(c for c in range(RENORM // 2, 65, RENORM // 2) if half_depth % c == 0)
    shape = (chunk, columns)
    lane = lax.broadcasted_iota(jnp.int32, shape, 1)
    order = (lax.rem(lane, GROUP) + group * GROUP) * plan.devices + me
    imaginary = lax.rem(lane // GROUP, 2) == 1
    keep = jnp.where((order == 0) & imaginary, 0.0, 1.0)
    offset = lax.broadcasted_iota(jnp.int32, shape, 0) * 2 + order
    own_row = lax.broadcasted_iota(jnp.int32, (GROUP, columns), 0)
    own_lane = lax.rem(lax.broadcasted_iota(jnp.int32, (GROUP, columns), 1), GROUP)
    own = jnp.where(own_row == own_lane, 1.0, 0.0)

    def over_shells(x):
        shift = 2 * GROUP
        while shift < columns:
            x = x + pltpu.roll(x, shift, 1)
            shift *= 2
        return x

    def rows_at(c):
        start = pl.multiple_of(half_at * GROUP + c * (chunk * GROUP), chunk * GROUP)
        return pl.ds(start, chunk * GROUP)

    def pick(values):
        return jnp.sum(values.reshape(chunk, GROUP, columns) * own[None], axis=1)

    def spread(values):
        wide = values[:, None, :] * own[None]
        return split_parts(wide.reshape(chunk * GROUP, columns))

    def degrees_at(c, parity):
        return pl.ds(plan.degree_at[group] + c * (2 * chunk) + parity, chunk, stride=2)

    def radial_at(c, parity):
        return jnp.exp((offset + (c * (2 * chunk) + parity)).astype(jnp.float32) * log_ratio)

    def add_adjoint(field, c, parity, weighted):
        rows = rows_at(c)
        top, low = spread(weighted)
        both = dot_atb(jnp.concatenate([top, low], axis=1), table_top[parity, rows, :])
        grid_ref[field, parity] += (
            both[:columns] + both[columns:] + dot_atb(top, table_low[parity, rows, :])
        )

    def first_pass(c, carry):
        rows = rows_at(c)
        tall = pl.ds(pl.multiple_of(c * chunk, chunk), chunk)
        terms = []
        for parity in range(2):
            top = table_top[parity, rows, :]
            terms.append(dot_abt(top, fold_top[parity]) + dot_abt(top, fold_low[parity])
                         + dot_abt(table_low[parity, rows, :], fold_top[parity]))
        for parity in range(2):
            radial = radial_at(c, parity)
            seen = seen_ref[degrees_at(c, parity), :]
            first = over_shells(pick(terms[parity][:, :columns]) * radial - seen)
            ahead = over_shells(pick(terms[parity][:, columns:]) * radial - seen)
            wanted_ref[parity, tall, :] = ahead
            add_adjoint(0, c, parity, radial * weight_ref[degrees_at(c, parity), :] * first)
        return carry

    def second_pass(c, carry):
        rows = rows_at(c)
        tall = pl.ds(pl.multiple_of(c * chunk, chunk), chunk)
        terms = []
        for parity in range(2):
            both = dot_abt(table_top[parity, rows, :], fold_top[parity])
            terms.append(both[:, :columns] + both[:, columns:]
                         + dot_abt(table_low[parity, rows, :], fold_top[parity, 0:columns, :]))
        for parity in range(2):
            radial = radial_at(c, parity)
            back = over_shells(pick(terms[parity]) * radial) * keep
            misfit = wanted_ref[parity, tall, :] - (0.5 * STEP * STEP) * back
            add_adjoint(1, c, parity, radial * weight_ref[degrees_at(c, parity), :] * misfit)
        return carry

    grid_ref[...] = jnp.zeros_like(grid_ref)
    lax.fori_loop(0, half_depth // chunk, first_pass, 0)
    for parity in range(2):
        top, low = split_parts(2.0 * grid_ref[0, parity])
        fold_top[parity, 0:columns, :] = top
        fold_top[parity, columns : 2 * columns, :] = low
    lax.fori_loop(0, half_depth // chunk, second_pass, 0)

    for field in range(2):
        even, odd = grid_ref[field, 0], grid_ref[field, 1]
        grid_ref[field, 0] = even + odd
        grid_ref[field, 1] = even - odd
    grids = [[grid_ref.at[field, side] for side in range(2)] for field in range(2)]
    scatter_fields(plan, group, grids, send_ref)


def misfit_kernel(plan, sent_ref, routed_ref, precision_ref, seed_ref, lat_ref, out_ref, recv_ref,
                  back_ref, pair_ref, owned_ref, table_top, table_low, fold_top, fold_low, wanted_ref,
                  grid_ref, weight_ref, seen_ref, send_sem, recv_sem, back_send_sem, back_recv_sem,
                  pair_sems, owned_sems):
    n, n_band = plan.devices, plan.n_band
    row, band = lax.axis_index("shell"), lax.axis_index("band")
    me = row * n_band + band
    barrier = pltpu.get_barrier_semaphore()

    def peer(i):
        to = lax.rem(me + i, n)
        return to, (to // n_band, lax.rem(to, n_band))

    def greet(i, carry):
        pl.semaphore_signal(barrier, inc=1, device_id=peer(i)[1], device_id_type=MESH)
        return carry

    def rows_of(group):
        end = plan.row_at[group + 1] if group + 1 < plan.groups else plan.rows
        return pl.ds(plan.row_at[group], end - plan.row_at[group])

    def start_group(group, source, target, sent_sems, got_sems):
        rows = rows_of(group)
        pltpu.make_async_copy(
            source.at[me, rows], target.at[me, rows], got_sems.at[group]
        ).start()

        def send(i, carry):
            to, device = peer(i)
            pltpu.make_async_remote_copy(
                src_ref=source.at[to, rows], dst_ref=target.at[me, rows],
                send_sem=sent_sems.at[group], recv_sem=got_sems.at[group],
                device_id=device, device_id_type=MESH,
            ).start()
            return carry

        lax.fori_loop(1, n, send, 0)

    def wait_for(ref, sem):
        pltpu.make_async_copy(ref, ref, sem).wait()

    lax.fori_loop(1, n, greet, 0)
    pl.semaphore_wait(barrier, n - 1)

    core, place, places = lax.rem(band, 2), band // 2, n_band // 2
    pair_copy = pltpu.make_async_remote_copy(
        src_ref=routed_ref.at[:, 1 - core], dst_ref=pair_ref, send_sem=pair_sems.at[0],
        recv_sem=pair_sems.at[1], device_id=(row, band + 1 - 2 * core), device_id_type=MESH,
    )
    pair_copy.start()
    start_group(plan.turns[0], sent_ref, recv_ref, send_sem, recv_sem)
    pair_copy.wait()
    pair_ref[...] += routed_ref[:, core]
    pltpu.make_async_copy(pair_ref.at[place], owned_ref.at[place], owned_sems.at[1]).start()

    def hand_over(i, carry):
        to = lax.rem(place + i, places)
        pltpu.make_async_remote_copy(
            src_ref=pair_ref.at[to], dst_ref=owned_ref.at[place], send_sem=owned_sems.at[0],
            recv_sem=owned_sems.at[1], device_id=(row, 2 * to + core), device_id_type=MESH,
        ).start()
        return carry

    lax.fori_loop(1, places, hand_over, 0)
    for group in plan.turns[1:]:
        start_group(group, sent_ref, recv_ref, send_sem, recv_sem)

    for group in range(plan.groups):
        legendre(plan, group, me, seed_ref, lat_ref, table_top, table_low)
    wait_for(owned_ref, owned_sems.at[1])
    total = owned_ref[0]
    for z in range(1, places):
        total = total + owned_ref[z]
    owned_ref[0] = total
    for group in range(plan.groups):
        degree_lanes(plan, group, me, precision_ref, owned_ref.at[0], weight_ref, seen_ref)

    lane = lax.broadcasted_iota(jnp.int32, (1, plan.columns), 1)
    for group in plan.turns:
        wait_for(recv_ref.at[:, rows_of(group)], recv_sem.at[group])
        if group == plan.turns[0]:
            ratio = jnp.ones((1, plan.columns), jnp.float32)
            for sy in range(plan.n_shell):
                for s in range(plan.local_shells):
                    at = plan.ratio_row + s
                    value = recv_ref[sy * n_band, at : at + 1, :]
                    ratio = jnp.where(lane // (2 * GROUP) == sy * plan.local_shells + s, value, ratio)
            log_ratio = jnp.log(ratio)
        misfit_group(plan, group, me, log_ratio, recv_ref, seen_ref, weight_ref, table_top, table_low,
                     fold_top, fold_low, wanted_ref, grid_ref, back_ref)
        start_group(group, back_ref, out_ref, back_send_sem, back_recv_sem)

    for group in range(plan.groups):
        rows = rows_of(group)
        wait_for(out_ref.at[:, rows], back_recv_sem.at[group])
        wait_for(sent_ref.at[pl.ds(0, n - 1), rows], send_sem.at[group])
        wait_for(back_ref.at[pl.ds(0, n - 1), rows], back_send_sem.at[group])
    if places > 1:
        wait_for(pair_ref.at[pl.ds(0, places - 1)], owned_sems.at[0])


def misfit(plan, sent, routed, precision, seed, lat):
    vmem = pl.BlockSpec(memory_space=pltpu.VMEM)
    table = pltpu.VMEM((2, plan.half_all * GROUP, plan.lat_lanes), jnp.bfloat16)
    fold = pltpu.VMEM((2, 2 * plan.columns, plan.lat_lanes), jnp.bfloat16)
    chunks = pltpu.VMEM(sent.shape, jnp.float32)
    owned = pltpu.VMEM((plan.n_band // 2, plan.seen_rows, LANES), jnp.float32)
    by_degree = pltpu.VMEM((plan.degree_all, plan.columns), jnp.float32)
    sems = lambda count: pltpu.SemaphoreType.DMA((count,))
    routed = routed.reshape(plan.n_band // 2, 2, plan.seen_rows, LANES)
    return pl.pallas_call(
        functools.partial(misfit_kernel, plan),
        out_shape=jax.ShapeDtypeStruct(sent.shape, sent.dtype),
        in_specs=[vmem] * 5,
        out_specs=vmem,
        scratch_shapes=[chunks, chunks, owned, owned, table, table, fold, fold,
                        pltpu.VMEM((2, plan.depth[0] // 2, plan.columns), jnp.float32),
                        pltpu.VMEM((2, 2, plan.columns, plan.lat_lanes), jnp.float32),
                        by_degree, by_degree]
        + [sems(plan.groups)] * 4 + [sems(2)] * 2,
        compiler_params=pltpu.CompilerParams(
            collective_id=0, has_side_effects=True, vmem_limit_bytes=VMEM_LIMIT
        ),
        name="misfit",
    )(sent, routed, precision, seed, lat)


def grids_kernel(plan, recv_ref, top_ref, low_ref, turn_ref, density_ref, momentum_ref, new_density_ref,
                 new_momentum_ref, total):
    step, g = pl.program_id(0), pl.program_id(1)
    south = (lax.axis_index("band") >= plan.n_band // 2).astype(jnp.int32)

    @pl.when((step == 0) & (g == 0))
    def _():
        total[...] = jnp.zeros_like(total)

    half = GROUP // 2
    for group in range(plan.groups):
        @pl.when(g == group)
        def _(group=group):
            row = plan.row_at[group]
            tiles = []
            for t in range(plan.tiles):
                if not plan.packed[group]:
                    tile = recv_ref[:, row + t * GROUP : row + (t + 1) * GROUP, :]
                else:
                    at = row + t // 2 * GROUP
                    tile = recv_ref[:, at : at + GROUP, :]
                    sub = lax.broadcasted_iota(jnp.int32, tile.shape, 1)
                    tile = jnp.where((sub < half) == (t % 2 == 0), tile, 0.0)
                tiles.append(tile.reshape(-1, LANES))
            for p, (first, last) in enumerate(plan.span):
                top, low = split_parts(jnp.concatenate(tiles[first:last], axis=1))
                table_top, table_low = top_ref[0, p], low_ref[0, p]
                total[p, 0 : (last - first) * LANES] += (
                    dot_atb(top, table_top) + dot_atb(low, table_top) + dot_atb(top, table_low)
                )

    @pl.when((step == pl.num_programs(0) - 1) & (g == plan.groups - 1))
    def _():
        grid = jnp.zeros((plan.wide, plan.lon_cells), jnp.float32)
        for p, (first, last) in enumerate(plan.span):
            start = p * plan.wide - first * LANES
            grid = grid + total[p, start : start + plan.wide]
        top, low = split_parts(grid)
        turn = turn_ref[south]
        grid = dot_ab(turn, top) + dot_ab(turn, low)
        density, momentum = density_ref[...], momentum_ref[...]
        half_momentum = momentum - 0.5 * STEP * (density + grid[: plan.cells])
        new_density = density + STEP * half_momentum
        new_density_ref[...] = new_density
        new_momentum_ref[...] = half_momentum - 0.5 * STEP * (new_density + grid[plan.cells :])


def grids(plan, returned, table, density, momentum):
    tall = min(plan.devices, 32)
    turn = jnp.asarray(plan.turn().astype(ml_dtypes.bfloat16))
    width = max(b - a for a, b in plan.span) * LANES
    whole = lambda shape: pl.BlockSpec(shape, lambda i, g: (0,) * len(shape))
    at_table = pl.BlockSpec((1, 2, tall * GROUP, plan.lon_cells), lambda i, g: (g, 0, i, 0))
    shape = jax.ShapeDtypeStruct(density.shape, jnp.float32)
    return pl.pallas_call(
        functools.partial(grids_kernel, plan),
        grid=(plan.devices // tall, plan.groups),
        in_specs=[pl.BlockSpec((tall, plan.rows, LANES), lambda i, g: (i, 0, 0)), at_table, at_table,
                  whole(turn.shape), whole(density.shape), whole(momentum.shape)],
        out_specs=[whole(density.shape)] * 2,
        out_shape=[shape, shape],
        scratch_shapes=[pltpu.VMEM((2, width, plan.lon_cells), jnp.float32)],
        compiler_params=pltpu.CompilerParams(vmem_limit_bytes=VMEM_LIMIT),
        name="grids",
    )(returned, table[0], table[1], turn, density, momentum)


def body(density, momentum, observed, order_list, shell_ratio, precision):
    slots, _, degrees = observed.shape
    local_shells, lat_rows, lon_cells = density.shape
    n_shell, n_band = lax.axis_size("shell"), lax.axis_size("band")
    plan = Plan(n_shell, n_band, local_shells, lat_rows, lon_cells, degrees)
    count = plan.groups * GROUP
    length = round_up(degrees, LANES) + LANES * -(-plan.devices // LANES)
    padded = jnp.pad(precision, (0, count * plan.devices + length))
    weight = jnp.stack([
        lax.slice_in_dim(padded, i * plan.devices, i * plan.devices + length) for i in range(count)
    ])
    orders = np.arange(count)[:, None] * plan.devices + np.arange(round_up(plan.devices, LANES))[None, :]
    order_value = jnp.asarray(np.minimum(orders, degrees).astype(np.float32))
    seed = 0.5 * (
        jnp.log(order_value + 0.5)
        + lax.lgamma(2.0 * order_value + 1.0)
        - order_value * jnp.log(4.0)
        - 2.0 * lax.lgamma(order_value + 1.0)
    )
    table = [jnp.asarray(x) for x in plan.fourier()]
    lat = jnp.asarray(plan.latitudes())
    ratio = jnp.broadcast_to(shell_ratio[:, None], (local_shells, LANES))
    flat_density = density.reshape(plan.cells, lon_cells)
    flat_momentum = momentum.reshape(plan.cells, lon_cells)
    sent, routed = spectra(plan, flat_density, flat_momentum, ratio, table,
                           order_list.reshape(n_band, slots), observed)
    returned = misfit(plan, sent, routed, weight, seed, lat)
    new_density, new_momentum = grids(plan, returned, table, flat_density, flat_momentum)
    return new_density.reshape(density.shape), new_momentum.reshape(density.shape)


def solution(mesh):
    in_specs = (
        P("shell", "band", None),
        P("shell", "band", None),
        P("band", None, None),
        P(),
        P("shell"),
        P(),
    )
    out_specs = (P("shell", "band", None), P("shell", "band", None))
    return jax.shard_map(body, mesh=mesh, in_specs=in_specs, out_specs=out_specs, check_vma=False)
```

```python
import functools

import jax
import jax.numpy as jnp
import ml_dtypes
import numpy as np
from jax import lax
from jax.experimental import pallas as pl
from jax.experimental.pallas import tpu as pltpu
from jax.sharding import PartitionSpec as P

STEP = 0.5
LANES = 128
GROUP = 8
RENORM = 16
MESH = pl.DeviceIdType.MESH
VMEM_LIMIT = 58 * 1024 * 1024


def dot_ab(a, b):
    return lax.dot_general(a, b, (((1,), (0,)), ((), ())), preferred_element_type=jnp.float32)


def dot_abt(a, b):
    return lax.dot_general(a, b, (((1,), (1,)), ((), ())), preferred_element_type=jnp.float32)


def dot_atb(a, b):
    return lax.dot_general(a, b, (((0,), (0,)), ((), ())), preferred_element_type=jnp.float32)


def split_parts(x):
    top = x.astype(jnp.bfloat16)
    return top, (x - top.astype(jnp.float32)).astype(jnp.bfloat16)


def round_up(x, to):
    return -(-x // to) * to


class Plan:
    def __init__(self, n_shell, n_band, local_shells, lat_rows, lon_cells, degrees):
        self.n_shell, self.n_band, self.local_shells = n_shell, n_band, local_shells
        self.lat_rows, self.lon_cells, self.degrees = lat_rows, lon_cells, degrees
        self.devices = n_shell * n_band
        self.shells = n_shell * local_shells
        self.lat_total = n_band * lat_rows
        self.cells = local_shells * lat_rows
        self.own = -(-degrees // self.devices)
        self.groups = -(-self.own // GROUP)
        self.wide = 2 * self.cells
        self.tiles = -(-2 * self.wide // LANES)
        self.span = [
            (p * self.wide // LANES, -(-(p + 1) * self.wide // LANES)) for p in range(2)
        ]
        self.turns = [self.groups - 1] + list(range(self.groups - 1))
        self.packed, self.row_at, rows = [], [], 0
        for g in range(self.groups):
            packed = self.own - g * GROUP <= GROUP // 2
            self.packed.append(packed)
            self.row_at.append(rows)
            used = self.tiles * (GROUP // 2 if packed else GROUP)
            if g == self.groups - 1:
                self.ratio_row = rows + used
                used += local_shells
            rows += round_up(used, 8)
        self.rows = rows
        self.depth = [
            min(degrees, round_up(degrees - g * GROUP * self.devices, 2 * RENORM))
            for g in range(self.groups)
        ]
        self.half_at = [sum(self.depth[:g]) // 2 for g in range(self.groups)]
        self.half_all = sum(self.depth) // 2
        pairs = n_band // 2
        self.per_block = max(q for q in range(1, pairs + 1) if pairs % q == 0 and q * lat_rows <= LANES)
        self.blocks = pairs // self.per_block
        self.lat_lanes = self.blocks * LANES
        self.columns = 2 * GROUP * self.shells
        self.degree_tiles = [round_up(depth, LANES) // LANES for depth in self.depth]
        self.degree_at = [sum(self.degree_tiles[:g]) * LANES for g in range(self.groups)]
        self.degree_all = sum(self.degree_tiles) * LANES
        self.seen_at = [2 * GROUP * sum(self.degree_tiles[:g]) for g in range(self.groups)]
        self.seen_rows = 2 * GROUP * sum(self.degree_tiles)

    def slot_of(self, g, i):
        return g * GROUP + (i % (GROUP // 2) if self.packed[g] else i)

    def fourier(self):
        n = np.arange(self.lon_cells)
        out = np.zeros((self.groups, 2, self.devices, GROUP, self.lon_cells), np.float32)
        for g in range(self.groups):
            for i in range(GROUP):
                slot = self.slot_of(g, i)
                if slot >= self.own:
                    continue
                order = slot * self.devices + np.arange(self.devices)
                live = order < self.degrees
                phase = (order[:, None] * n[None, :]) % self.lon_cells * (2.0 * np.pi / self.lon_cells)
                factor = np.where(order == 0, 1.0, np.sqrt(2.0)) * live / np.sqrt(self.lon_cells)
                out[g, 0, :, i] = factor[:, None] * np.cos(phase)
                out[g, 1, :, i] = -factor[:, None] * np.sin(phase)
        out = out.reshape(self.groups, 2, self.devices * GROUP, self.lon_cells)
        top = out.astype(ml_dtypes.bfloat16)
        low = (out - top.astype(np.float32)).astype(ml_dtypes.bfloat16)
        return top, low

    def turn(self):
        at = np.arange(self.wide)
        back = at // self.lat_rows * self.lat_rows + (self.lat_rows - 1 - at % self.lat_rows)
        return np.stack([at[:, None] == at[None, :], at[:, None] == back[None, :]])

    def placement(self):
        turn = self.turn()
        width = max(b - a for a, b in self.span) * LANES
        out = np.zeros((2, 2, width, self.wide), bool)
        for p in range(2):
            start = p * self.wide - self.span[p][0] * LANES
            out[:, p, start : start + self.wide] = turn
        return out.astype(ml_dtypes.bfloat16)

    def latitudes(self):
        lane = np.arange(self.lat_lanes)
        inside = lane % LANES
        live = inside < self.per_block * self.lat_rows
        row = lane // LANES * (self.per_block * self.lat_rows) + np.where(live, inside, 0)
        angle = (row.astype(np.float32) + np.float32(0.5)) * np.float32(np.pi / self.lat_total)
        angle = angle.astype(np.float32).astype(np.float64)
        sine = np.sin(angle).astype(np.float32)
        quadrature = np.sqrt(sine * np.float32(np.pi / self.lat_total)) * live
        rows = np.zeros((8, self.lat_lanes), np.float32)
        rows[0] = np.cos(angle)
        rows[1] = np.log(sine.astype(np.float64))
        rows[2] = quadrature
        return rows


def route_observed(plan, orders_ref, observed_ref, routed_ref):
    slots = plan.groups * GROUP
    row, band = lax.axis_index("shell"), lax.axis_index("band")
    held = observed_ref.shape[0]
    lane = lax.broadcasted_iota(jnp.int32, (1, round_up(held, LANES)), 1)

    def read(t, orders):
        return jnp.where(lane == t, orders_ref[band * held + t], orders)

    orders = lax.fori_loop(0, held, read, jnp.full(lane.shape, plan.degrees, jnp.int32))
    orders = orders[:, :held]
    shape = (plan.n_band, slots, held)
    slot = lax.broadcasted_iota(jnp.int32, shape, 1)
    owner = lax.broadcasted_iota(jnp.int32, shape, 0) + row * plan.n_band
    wanted = slot * plan.devices + owner
    wanted = jnp.where((slot < plan.own) & (wanted < plan.degrees), wanted, -1)
    chosen = jnp.where(wanted == orders[None], 1.0, 0.0).reshape(plan.n_band * slots, -1)
    chosen = chosen.astype(jnp.bfloat16)
    for p in range(2):
        top, low = split_parts(observed_ref[:, p, :])
        rows = (dot_ab(chosen, top) + dot_ab(chosen, low)).reshape(
            plan.n_band // 2, 2, slots, plan.degrees
        )
        for g in range(plan.groups):
            for t in range(plan.degree_tiles[g]):
                at = plan.seen_at[g] + (p * plan.degree_tiles[g] + t) * GROUP
                routed_ref[:, :, at : at + GROUP, :] = rows[
                    :, :, g * GROUP : (g + 1) * GROUP, t * LANES : (t + 1) * LANES
                ]


def place_fields(plan, south, density_ref, momentum_ref, place_ref, field_top, field_low):
    density = density_ref[...]
    ahead = (1.0 - 0.5 * STEP * STEP) * density + STEP * momentum_ref[...]
    top, low = split_parts(jnp.concatenate([density, ahead], axis=0))
    for p in range(2):
        place = place_ref[south, p]
        field_top[p] = dot_ab(place, top).astype(jnp.bfloat16)
        field_low[p] = dot_ab(place, low).astype(jnp.bfloat16)


def spectra(plan, group, field_top, field_low, top_ref, low_ref, ratio_ref, out_ref):
    parts = []
    for p in range(2):
        table_top = top_ref[p]
        parts.append(
            dot_abt(table_top, field_top[p]) + dot_abt(table_top, field_low[p])
            + dot_abt(low_ref[p], field_top[p])
        )
    tiles = []
    for t in range(plan.tiles):
        tile = None
        for p, (first, last) in enumerate(plan.span):
            if first <= t < last:
                piece = parts[p][:, (t - first) * LANES : (t - first + 1) * LANES]
                tile = piece if tile is None else tile + piece
        tiles.append(tile.reshape(-1, GROUP, LANES))
    row, half = plan.row_at[group], GROUP // 2
    if not plan.packed[group]:
        for t in range(plan.tiles):
            out_ref[:, row + t * GROUP : row + (t + 1) * GROUP, :] = tiles[t]
    else:
        sub = lax.broadcasted_iota(jnp.int32, tiles[0].shape, 1)
        for t in range(0, plan.tiles - 1, 2):
            out_ref[:, row + t * half : row + t * half + GROUP, :] = jnp.where(
                sub < half, tiles[t], tiles[t + 1]
            )
        if plan.tiles % 2:
            t = plan.tiles - 1
            out_ref[:, row + t * half : row + (t + 1) * half, :] = tiles[t][:, :half]
    if group == plan.groups - 1:
        for s in range(plan.local_shells):
            at = plan.ratio_row + s
            out_ref[:, at : at + 1, :] = jnp.full((plan.devices, 1, LANES), ratio_ref[s], jnp.float32)
        spare = plan.rows - plan.ratio_row - plan.local_shells
        if spare:
            out_ref[:, plan.rows - spare :, :] = jnp.zeros((plan.devices, spare, LANES), jnp.float32)


def add_grids(plan, group, recv_ref, top_ref, low_ref, total):
    row, half = plan.row_at[group], GROUP // 2
    tiles = []
    for t in range(plan.tiles):
        if not plan.packed[group]:
            tile = recv_ref[:, row + t * GROUP : row + (t + 1) * GROUP, :]
        else:
            at = row + t // 2 * GROUP
            tile = recv_ref[:, at : at + GROUP, :]
            sub = lax.broadcasted_iota(jnp.int32, tile.shape, 1)
            tile = jnp.where((sub < half) == (t % 2 == 0), tile, 0.0)
        tiles.append(tile.reshape(-1, LANES))
    for p, (first, last) in enumerate(plan.span):
        top, low = split_parts(jnp.concatenate(tiles[first:last], axis=1))
        table_top = top_ref[p]
        value = dot_atb(top, table_top) + dot_atb(low, table_top) + dot_atb(top, low_ref[p])
        start = p * plan.wide - first * LANES
        total[...] += value[start : start + plan.wide]


def finish(plan, south, total, turn_ref, density_ref, momentum_ref, new_density_ref, new_momentum_ref):
    top, low = split_parts(total[...])
    turn = turn_ref[south]
    grid = dot_ab(turn, top) + dot_ab(turn, low)
    density, momentum = density_ref[...], momentum_ref[...]
    half_momentum = momentum - 0.5 * STEP * (density + grid[: plan.cells])
    new_density = density + STEP * half_momentum
    new_density_ref[...] = new_density
    new_momentum_ref[...] = half_momentum - 0.5 * STEP * (new_density + grid[plan.cells :])


def legendre(plan, group, me, seed_ref, lat_ref, table_top, table_low):
    shape = (GROUP, LANES)
    slot = lax.broadcasted_iota(jnp.int32, shape, 0) + group * GROUP
    lane = lax.broadcasted_iota(jnp.int32, shape, 1)
    order = slot * plan.devices + me
    live = (slot < plan.own) & (order < plan.degrees)
    order = jnp.where(live, order, plan.degrees)
    order_value = order.astype(jnp.float32)
    depth = plan.depth[group]
    growths, dampings = [], []
    for t in range(-(-depth // LANES)):
        step_int = lane + (t * LANES + 1)
        step = step_int.astype(jnp.float32)
        total = order_value + step
        growth = jnp.sqrt((4.0 * total * total - 1.0) / (step * (2.0 * order_value + step)))
        growths.append(jnp.where(order + step_int < plan.degrees, growth, 0.0))
        lower = (total - 1.0) * (total - 1.0)
        dampings.append(jnp.sqrt(
            (step - 1.0) * (2.0 * order_value + step - 1.0) / jnp.maximum(4.0 * lower - 1.0, 1.0)
        ))
    full = (GROUP, plan.lat_lanes)
    cosine = jnp.broadcast_to(lat_ref[0:1, :], full)
    quadrature = jnp.broadcast_to(lat_ref[2:3, :], full)
    seed = seed_ref[group * GROUP : (group + 1) * GROUP, :]
    device = lax.broadcasted_iota(jnp.int32, seed.shape, 1)
    seed = jnp.sum(jnp.where(device == me, seed, 0.0), axis=1, keepdims=True)
    orders = order_value[:, 0:1]
    log_value = orders * lat_ref[1:2, :] + seed
    current = jnp.where(orders < plan.degrees, jnp.ones(full, jnp.float32), 0.0)
    previous = jnp.zeros(full, jnp.float32)
    per_tile = LANES // RENORM

    for t in range(-(-depth // LANES)):
        count = min(per_tile, (depth - t * LANES) // RENORM)
        half_start = plan.half_at[group] * GROUP

        def one_span(i, carry, t=t):
            current, previous, log_value = carry
            factor = jnp.exp(log_value) * quadrature
            shift = lax.rem(LANES - i * RENORM, LANES)
            growth_tile = pltpu.roll(growths[t], shift, 1)
            damping_tile = pltpu.roll(dampings[t], shift, 1)
            values = [[], []]
            for step in range(RENORM):
                values[step % 2].append(current * factor)
                growth = growth_tile[:, step : step + 1]
                damping = damping_tile[:, step : step + 1]
                current, previous = growth * (cosine * current - damping * previous), current
            largest = jnp.maximum(jnp.abs(current), jnp.abs(previous))
            largest = jnp.where(largest == 0.0, 1.0, largest)
            row = half_start + (t * per_tile + i) * (RENORM // 2 * GROUP)
            row = pl.multiple_of(row, RENORM // 2 * GROUP)
            for parity in range(2):
                top, low = split_parts(jnp.concatenate(values[parity], axis=0))
                table_top[parity, pl.ds(row, RENORM // 2 * GROUP), :] = top
                table_low[parity, pl.ds(row, RENORM // 2 * GROUP), :] = low
            return current / largest, previous / largest, log_value + jnp.log(largest)

        current, previous, log_value = lax.fori_loop(0, count, one_span, (current, previous, log_value))


def moved(tiles, start, width, dest):
    first, offset = start // LANES, start % LANES
    shift = (dest - offset) % LANES
    turn = lambda x: pltpu.roll(x, shift, 1) if shift else x
    value = turn(tiles[first])
    if offset + width > LANES:
        lane = lax.broadcasted_iota(jnp.int32, value.shape, 1)
        value = jnp.where(lane < dest + LANES - offset, value, turn(tiles[first + 1]))
    return value


def gather_fields(plan, group, recv_ref, fold_top, fold_low):
    row, half = plan.row_at[group], GROUP // 2

    def tiles_of(device):
        out = []
        for t in range(plan.tiles):
            if not plan.packed[group]:
                out.append(recv_ref[device, row + t * GROUP : row + (t + 1) * GROUP, :])
            else:
                at = row + t // 2 * GROUP
                pair = recv_ref[device, at : at + GROUP, :]
                out.append(pltpu.roll(pair, half, 0) if t % 2 else pair)
        return out

    lane = lax.broadcasted_iota(jnp.int32, (GROUP, LANES), 1)
    width = plan.lat_rows
    for sy in range(plan.n_shell):
        for block in range(plan.blocks):
            sides = {}
            for inside in range(plan.per_block):
                band = block * plan.per_block + inside
                for side, source in enumerate((band, plan.n_band - 1 - band)):
                    tiles = tiles_of(sy * plan.n_band + source)
                    for piece in range(4 * plan.local_shells):
                        value = moved(tiles, piece * width, width, inside * width)
                        if inside:
                            value = jnp.where(lane < inside * width, sides[side, piece], value)
                        sides[side, piece] = value
            for field in range(2):
                for s in range(plan.local_shells):
                    pieces = [(p * 2 + field) * plan.local_shells + s for p in range(2)]
                    north = jnp.concatenate([sides[0, at] for at in pieces], axis=0)
                    south = jnp.concatenate([sides[1, at] for at in pieces], axis=0)
                    start = field * plan.columns + (sy * plan.local_shells + s) * 2 * GROUP
                    for parity, folded in enumerate((north + south, north - south)):
                        top, low = split_parts(folded)
                        at = (parity, pl.ds(start, 2 * GROUP), pl.ds(block * LANES, LANES))
                        fold_top[at] = top
                        fold_low[at] = low


def scatter_fields(plan, group, grids, send_ref):
    row, half, width = plan.row_at[group], GROUP // 2, plan.lat_rows
    lane = lax.broadcasted_iota(jnp.int32, (GROUP, LANES), 1)
    sub = lax.broadcasted_iota(jnp.int32, (GROUP, LANES), 0)
    for sy in range(plan.n_shell):
        for band in range(plan.n_band):
            side = int(band >= plan.n_band // 2)
            mirrored = plan.n_band - 1 - band if side else band
            block, inside = mirrored // plan.per_block, mirrored % plan.per_block
            tiles = []
            for t in range(plan.tiles):
                tile = None
                for piece in range(4 * plan.local_shells):
                    start = piece * width - t * LANES
                    if start + width <= 0 or start >= LANES:
                        continue
                    p, field, s = piece // (2 * plan.local_shells), piece // plan.local_shells % 2, piece % plan.local_shells
                    at = ((sy * plan.local_shells + s) * 2 + p) * GROUP
                    value = grids[field][side][at : at + GROUP, pl.ds(block * LANES, LANES)]
                    shift = (start - inside * width) % LANES
                    if shift:
                        value = pltpu.roll(value, shift, 1)
                    tile = value if tile is None else jnp.where(lane < start, tile, value)
                tiles.append(tile)
            device = sy * plan.n_band + band
            if not plan.packed[group]:
                for t in range(plan.tiles):
                    send_ref[device, row + t * GROUP : row + (t + 1) * GROUP, :] = tiles[t]
            else:
                for t in range(0, plan.tiles, 2):
                    pair = tiles[t]
                    if t + 1 < plan.tiles:
                        pair = jnp.where(sub < half, pair, pltpu.roll(tiles[t + 1], half, 0))
                    send_ref[device, row + t * half : row + t * half + GROUP, :] = pair


def degree_lanes(plan, group, me, precision_ref, total, weight_ref, seen_ref):
    width = round_up(plan.groups * GROUP * plan.devices + plan.degrees, LANES)
    row = jnp.concatenate(
        [precision_ref[...], jnp.zeros((1, width - plan.degrees), jnp.float32)], axis=1
    )
    row = jnp.broadcast_to(row, (GROUP, width))
    sub = lax.broadcasted_iota(jnp.int32, (GROUP, width), 0)
    precision = row
    for i in range(GROUP):
        start = (group * GROUP + i) * plan.devices
        precision = jnp.where(sub == i, pltpu.roll(row, (width - start) % width, 1), precision)
    precision = pltpu.roll(precision, lax.rem(width - me, width), 1)
    copies = plan.columns // GROUP
    nothing = jnp.zeros((plan.columns - 2 * GROUP, LANES), jnp.float32)
    for t in range(plan.degree_tiles[group]):
        rows = pl.ds(plan.degree_at[group] + t * LANES, LANES)
        tile = precision[:, t * LANES : (t + 1) * LANES]
        weight_ref[rows, :] = jnp.concatenate([tile] * copies, axis=0).T
        tiles = []
        for p in range(2):
            at = plan.seen_at[group] + (p * plan.degree_tiles[group] + t) * GROUP
            tiles.append(total[at : at + GROUP, :])
        seen_ref[rows, :] = jnp.concatenate(tiles + [nothing], axis=0).T


def misfit_group(plan, group, me, log_ratio, recv_ref, seen_ref, weight_ref, table_top, table_low,
                 fold_top, fold_low, wanted_ref, grid_ref, send_ref):
    columns = plan.columns
    gather_fields(plan, group, recv_ref, fold_top, fold_low)
    half_depth = plan.depth[group] // 2
    half_at = plan.half_at[group]
    chunk = max(c for c in range(RENORM // 2, 65, RENORM // 2) if half_depth % c == 0)
    shape = (chunk, columns)
    lane = lax.broadcasted_iota(jnp.int32, shape, 1)
    order = (lax.rem(lane, GROUP) + group * GROUP) * plan.devices + me
    imaginary = lax.rem(lane // GROUP, 2) == 1
    keep = jnp.where((order == 0) & imaginary, 0.0, 1.0)
    offset = lax.broadcasted_iota(jnp.int32, shape, 0) * 2 + order
    own_row = lax.broadcasted_iota(jnp.int32, (GROUP, columns), 0)
    own_lane = lax.rem(lax.broadcasted_iota(jnp.int32, (GROUP, columns), 1), GROUP)
    own = jnp.where(own_row == own_lane, 1.0, 0.0)

    def over_shells(x):
        shift = 2 * GROUP
        while shift < columns:
            x = x + pltpu.roll(x, shift, 1)
            shift *= 2
        return x

    def rows_at(c):
        start = pl.multiple_of(half_at * GROUP + c * (chunk * GROUP), chunk * GROUP)
        return pl.ds(start, chunk * GROUP)

    def pick(values):
        return jnp.sum(values.reshape(chunk, GROUP, columns) * own[None], axis=1)

    def spread(values):
        wide = values[:, None, :] * own[None]
        return split_parts(wide.reshape(chunk * GROUP, columns))

    def degrees_at(c, parity):
        return pl.ds(plan.degree_at[group] + c * (2 * chunk) + parity, chunk, stride=2)

    def radial_at(c, parity):
        return jnp.exp((offset + (c * (2 * chunk) + parity)).astype(jnp.float32) * log_ratio)

    def add_adjoint(field, c, parity, weighted):
        rows = rows_at(c)
        top, low = spread(weighted)
        both = dot_atb(jnp.concatenate([top, low], axis=1), table_top[parity, rows, :])
        grid_ref[field, parity] += (
            both[:columns] + both[columns:] + dot_atb(top, table_low[parity, rows, :])
        )

    def first_pass(c, carry):
        rows = rows_at(c)
        tall = pl.ds(pl.multiple_of(c * chunk, chunk), chunk)
        terms = []
        for parity in range(2):
            top = table_top[parity, rows, :]
            terms.append(dot_abt(top, fold_top[parity]) + dot_abt(top, fold_low[parity])
                         + dot_abt(table_low[parity, rows, :], fold_top[parity]))
        for parity in range(2):
            radial = radial_at(c, parity)
            seen = seen_ref[degrees_at(c, parity), :]
            first = over_shells(pick(terms[parity][:, :columns]) * radial - seen)
            ahead = over_shells(pick(terms[parity][:, columns:]) * radial - seen)
            wanted_ref[parity, tall, :] = ahead
            add_adjoint(0, c, parity, radial * weight_ref[degrees_at(c, parity), :] * first)
        return carry

    def second_pass(c, carry):
        rows = rows_at(c)
        tall = pl.ds(pl.multiple_of(c * chunk, chunk), chunk)
        terms = []
        for parity in range(2):
            both = dot_abt(table_top[parity, rows, :], fold_top[parity])
            terms.append(both[:, :columns] + both[:, columns:]
                         + dot_abt(table_low[parity, rows, :], fold_top[parity, 0:columns, :]))
        for parity in range(2):
            radial = radial_at(c, parity)
            back = over_shells(pick(terms[parity]) * radial) * keep
            misfit = wanted_ref[parity, tall, :] - (0.5 * STEP * STEP) * back
            add_adjoint(1, c, parity, radial * weight_ref[degrees_at(c, parity), :] * misfit)
        return carry

    grid_ref[...] = jnp.zeros_like(grid_ref)
    lax.fori_loop(0, half_depth // chunk, first_pass, 0)
    for parity in range(2):
        top, low = split_parts(2.0 * grid_ref[0, parity])
        fold_top[parity, 0:columns, :] = top
        fold_top[parity, columns : 2 * columns, :] = low
    lax.fori_loop(0, half_depth // chunk, second_pass, 0)

    for field in range(2):
        even, odd = grid_ref[field, 0], grid_ref[field, 1]
        grid_ref[field, 0] = even + odd
        grid_ref[field, 1] = even - odd
    grids = [[grid_ref.at[field, side] for side in range(2)] for field in range(2)]
    scatter_fields(plan, group, grids, send_ref)


def step_kernel(plan, density_ref, momentum_ref, place_ref, turn_ref, observed_ref, precision_ref,
                seed_ref, lat_ref, orders_ref, ratio_ref, top_hbm, low_hbm, new_density_ref,
                new_momentum_ref, fourier_top, fourier_low, field_top, field_low, total_ref, sent_ref,
                recv_ref, back_ref, out_ref, routed_ref, pair_ref, owned_ref, table_top, table_low,
                fold_top, fold_low, wanted_ref, grid_ref, weight_ref, seen_ref, load_sems, send_sem,
                recv_sem, back_send_sem, back_recv_sem, pair_sems, owned_sems):
    n, n_band = plan.devices, plan.n_band
    row, band = lax.axis_index("shell"), lax.axis_index("band")
    me = row * n_band + band
    south = (band >= n_band // 2).astype(jnp.int32)
    barrier = pltpu.get_barrier_semaphore()

    def peer(i):
        to = lax.rem(me + i, n)
        return to, (to // n_band, lax.rem(to, n_band))

    def greet(i, carry):
        pl.semaphore_signal(barrier, inc=1, device_id=peer(i)[1], device_id_type=MESH)
        return carry

    def rows_of(group):
        end = plan.row_at[group + 1] if group + 1 < plan.groups else plan.rows
        return pl.ds(plan.row_at[group], end - plan.row_at[group])

    def start_group(group, source, target, sent_sems, got_sems):
        rows = rows_of(group)
        pltpu.make_async_copy(
            source.at[me, rows], target.at[me, rows], got_sems.at[group]
        ).start()

        def send(i, carry):
            to, device = peer(i)
            pltpu.make_async_remote_copy(
                src_ref=source.at[to, rows], dst_ref=target.at[me, rows],
                send_sem=sent_sems.at[group], recv_sem=got_sems.at[group],
                device_id=device, device_id_type=MESH,
            ).start()
            return carry

        lax.fori_loop(1, n, send, 0)

    def wait_for(ref, sem):
        pltpu.make_async_copy(ref, ref, sem).wait()

    def load(group, part):
        source, target = ((top_hbm, fourier_top), (low_hbm, fourier_low))[part]
        return pltpu.make_async_copy(source.at[group], target.at[group], load_sems.at[group, part])

    for group in plan.turns:
        for part in range(2):
            load(group, part).start()
    lax.fori_loop(1, n, greet, 0)
    place_fields(plan, south, density_ref, momentum_ref, place_ref, field_top, field_low)

    core, place, places = lax.rem(band, 2), band // 2, n_band // 2
    pair_copy = pltpu.make_async_remote_copy(
        src_ref=routed_ref.at[:, 1 - core], dst_ref=pair_ref, send_sem=pair_sems.at[0],
        recv_sem=pair_sems.at[1], device_id=(row, band + 1 - 2 * core), device_id_type=MESH,
    )

    def hand_over(i, carry):
        to = lax.rem(place + i, places)
        pltpu.make_async_remote_copy(
            src_ref=pair_ref.at[to], dst_ref=owned_ref.at[place], send_sem=owned_sems.at[0],
            recv_sem=owned_sems.at[1], device_id=(row, 2 * to + core), device_id_type=MESH,
        ).start()
        return carry

    def share_observed():
        pair_copy.wait()
        pair_ref[...] += routed_ref[:, core]
        pltpu.make_async_copy(pair_ref.at[place], owned_ref.at[place], owned_sems.at[1]).start()
        lax.fori_loop(1, places, hand_over, 0)

    for turn, group in enumerate(plan.turns):
        for part in range(2):
            load(group, part).wait()
        spectra(plan, group, field_top, field_low, fourier_top.at[group], fourier_low.at[group],
                ratio_ref, sent_ref)
        if turn == 0:
            pl.semaphore_wait(barrier, n - 1)
        start_group(group, sent_ref, recv_ref, send_sem, recv_sem)
        if turn == 0:
            route_observed(plan, orders_ref, observed_ref, routed_ref)
            pair_copy.start()
        if turn == 1:
            share_observed()
    if plan.groups == 1:
        share_observed()

    for group in plan.turns:
        legendre(plan, group, me, seed_ref, lat_ref, table_top, table_low)
    wait_for(owned_ref, owned_sems.at[1])
    owned = owned_ref[0]
    for z in range(1, places):
        owned = owned + owned_ref[z]
    owned_ref[0] = owned
    for group in range(plan.groups):
        degree_lanes(plan, group, me, precision_ref, owned_ref.at[0], weight_ref, seen_ref)

    lane = lax.broadcasted_iota(jnp.int32, (1, plan.columns), 1)
    for group in plan.turns:
        wait_for(recv_ref.at[:, rows_of(group)], recv_sem.at[group])
        if group == plan.turns[0]:
            ratio = jnp.ones((1, plan.columns), jnp.float32)
            for sy in range(plan.n_shell):
                for s in range(plan.local_shells):
                    at = plan.ratio_row + s
                    value = recv_ref[sy * n_band, at : at + 1, :]
                    ratio = jnp.where(lane // (2 * GROUP) == sy * plan.local_shells + s, value, ratio)
            log_ratio = jnp.log(ratio)
        misfit_group(plan, group, me, log_ratio, recv_ref, seen_ref, weight_ref, table_top, table_low,
                     fold_top, fold_low, wanted_ref, grid_ref, back_ref)
        start_group(group, back_ref, out_ref, back_send_sem, back_recv_sem)

    total_ref[...] = jnp.zeros_like(total_ref)
    for group in plan.turns:
        wait_for(out_ref.at[:, rows_of(group)], back_recv_sem.at[group])
        add_grids(plan, group, out_ref, fourier_top.at[group], fourier_low.at[group], total_ref)
    finish(plan, south, total_ref, turn_ref, density_ref, momentum_ref, new_density_ref,
           new_momentum_ref)

    for group in range(plan.groups):
        rows = rows_of(group)
        wait_for(sent_ref.at[pl.ds(0, n - 1), rows], send_sem.at[group])
        wait_for(back_ref.at[pl.ds(0, n - 1), rows], back_send_sem.at[group])
    if places > 1:
        wait_for(pair_ref.at[pl.ds(0, places - 1)], owned_sems.at[0])


def step(plan, density, momentum, observed, precision, seed, orders, ratio):
    vmem = pl.BlockSpec(memory_space=pltpu.VMEM)
    smem = pl.BlockSpec(memory_space=pltpu.SMEM)
    hbm = pl.BlockSpec(memory_space=pl.ANY)
    fourier = [jnp.asarray(x) for x in plan.fourier()]
    placement = jnp.asarray(plan.placement())
    turn = jnp.asarray(plan.turn().astype(ml_dtypes.bfloat16))
    f32, bf16 = jnp.float32, jnp.bfloat16
    field = pltpu.VMEM((2, placement.shape[2], plan.lon_cells), bf16)
    chunks = pltpu.VMEM((plan.devices, plan.rows, LANES), f32)
    routed = pltpu.VMEM((plan.n_band // 2, 2, plan.seen_rows, LANES), f32)
    owned = pltpu.VMEM((plan.n_band // 2, plan.seen_rows, LANES), f32)
    table = pltpu.VMEM((2, plan.half_all * GROUP, plan.lat_lanes), bf16)
    fold = pltpu.VMEM((2, 2 * plan.columns, plan.lat_lanes), bf16)
    by_degree = pltpu.VMEM((plan.degree_all, plan.columns), f32)
    sems = lambda *count: pltpu.SemaphoreType.DMA(count)
    shape = jax.ShapeDtypeStruct(density.shape, f32)
    return pl.pallas_call(
        functools.partial(step_kernel, plan),
        out_shape=[shape, shape],
        in_specs=[vmem] * 8 + [smem] * 2 + [hbm] * 2,
        out_specs=[vmem] * 2,
        scratch_shapes=[pltpu.VMEM(fourier[0].shape, bf16)] * 2
        + [field] * 2 + [pltpu.VMEM((plan.wide, plan.lon_cells), f32)] + [chunks] * 4
        + [routed, owned, owned, table, table, fold, fold,
           pltpu.VMEM((2, plan.depth[0] // 2, plan.columns), f32),
           pltpu.VMEM((2, 2, plan.columns, plan.lat_lanes), f32), by_degree, by_degree]
        + [sems(plan.groups, 2)] + [sems(plan.groups)] * 4 + [sems(2)] * 2,
        compiler_params=pltpu.CompilerParams(
            collective_id=0, has_side_effects=True, vmem_limit_bytes=VMEM_LIMIT
        ),
        name="step",
    )(density, momentum, placement, turn, observed, precision, seed, jnp.asarray(plan.latitudes()),
      orders, ratio, *fourier)


def body(density, momentum, observed, order_list, shell_ratio, precision):
    slots, _, degrees = observed.shape
    local_shells, lat_rows, lon_cells = density.shape
    n_shell, n_band = lax.axis_size("shell"), lax.axis_size("band")
    plan = Plan(n_shell, n_band, local_shells, lat_rows, lon_cells, degrees)
    count = plan.groups * GROUP
    orders = np.arange(count)[:, None] * plan.devices + np.arange(round_up(plan.devices, LANES))[None, :]
    order_value = jnp.asarray(np.minimum(orders, degrees).astype(np.float32))
    seed = 0.5 * (
        jnp.log(order_value + 0.5)
        + lax.lgamma(2.0 * order_value + 1.0)
        - order_value * jnp.log(4.0)
        - 2.0 * lax.lgamma(order_value + 1.0)
    )
    new_density, new_momentum = step(
        plan, density.reshape(plan.cells, lon_cells), momentum.reshape(plan.cells, lon_cells),
        observed, precision.reshape(1, degrees), seed, order_list, shell_ratio,
    )
    return new_density.reshape(density.shape), new_momentum.reshape(density.shape)


def solution(mesh):
    in_specs = (
        P("shell", "band", None),
        P("shell", "band", None),
        P("band", None, None),
        P(),
        P("shell"),
        P(),
    )
    out_specs = (P("shell", "band", None), P("shell", "band", None))
    return jax.shard_map(body, mesh=mesh, in_specs=in_specs, out_specs=out_specs, check_vma=False)
```

```python
import functools

import jax
import jax.numpy as jnp
import ml_dtypes
import numpy as np
from jax import lax
from jax.experimental import pallas as pl
from jax.experimental.pallas import tpu as pltpu
from jax.sharding import PartitionSpec as P

STEP = 0.5
LANES = 128
GROUP = 8
RENORM = 16
MESH = pl.DeviceIdType.MESH
VMEM_LIMIT = 58 * 1024 * 1024


def dot_ab(a, b):
    return lax.dot_general(a, b, (((1,), (0,)), ((), ())), preferred_element_type=jnp.float32)


def dot_abt(a, b):
    return lax.dot_general(a, b, (((1,), (1,)), ((), ())), preferred_element_type=jnp.float32)


def dot_atb(a, b):
    return lax.dot_general(a, b, (((0,), (0,)), ((), ())), preferred_element_type=jnp.float32)


def split_parts(x):
    top = x.astype(jnp.bfloat16)
    return top, (x - top.astype(jnp.float32)).astype(jnp.bfloat16)


def round_up(x, to):
    return -(-x // to) * to


class Plan:
    def __init__(self, n_shell, n_band, local_shells, lat_rows, lon_cells, degrees):
        self.n_shell, self.n_band, self.local_shells = n_shell, n_band, local_shells
        self.lat_rows, self.lon_cells, self.degrees = lat_rows, lon_cells, degrees
        self.devices = n_shell * n_band
        self.shells = n_shell * local_shells
        self.lat_total = n_band * lat_rows
        self.cells = local_shells * lat_rows
        full = degrees // (GROUP * self.devices)
        rest = degrees - full * GROUP * self.devices
        self.groups = full + (rest > 0)
        self.halved = full > 0 and 0 < rest <= min(GROUP * self.devices // 2, 2 * LANES // 2)
        self.half_devices = self.devices // 2
        self.base = [g * GROUP * self.devices for g in range(self.groups)]
        self.stride = [self.devices] * self.groups
        if self.halved:
            self.stride[-1] = self.half_devices
        self.table_at = [GROUP * sum(self.stride[:g]) for g in range(self.groups)]
        self.table_rows = GROUP * sum(self.stride)
        self.wide = 2 * self.cells
        self.tiles = -(-2 * self.wide // LANES)
        self.span = [
            (p * self.wide // LANES, -(-(p + 1) * self.wide // LANES)) for p in range(2)
        ]
        self.turns = [self.groups - 1] + list(range(self.groups - 1))
        self.row_at, rows = [], 0
        for g in range(self.groups):
            self.row_at.append(rows)
            used = self.tiles * GROUP
            if g == self.groups - 1:
                self.ratio_row = rows + used
                used += local_shells
            rows += round_up(used, 8)
        self.rows = rows
        self.depth = [
            min(degrees, round_up(degrees - base, 2 * RENORM)) for base in self.base
        ]
        self.half_at = [sum(self.depth[:g]) // 2 for g in range(self.groups)]
        self.half_all = sum(self.depth) // 2
        pairs = n_band // 2
        self.per_block = max(q for q in range(1, pairs + 1) if pairs % q == 0 and q * lat_rows <= LANES)
        self.blocks = pairs // self.per_block
        self.lat_lanes = self.blocks * LANES
        self.columns = 2 * GROUP * self.shells
        self.degree_tiles = [round_up(depth, LANES) // LANES for depth in self.depth]
        self.degree_at = [sum(self.degree_tiles[:g]) * LANES for g in range(self.groups)]
        self.degree_all = sum(self.degree_tiles) * LANES
        self.seen_at = [2 * GROUP * sum(self.degree_tiles[:g]) for g in range(self.groups)]
        self.seen_rows = 2 * GROUP * sum(self.degree_tiles)

    def is_half(self, g):
        return self.halved and g == self.groups - 1

    def order(self, g, slot, owner):
        return self.base[g] + slot * self.stride[g] + owner

    def owner(self, g, row, band):
        if self.is_half(g):
            south = (band >= self.n_band // 2) * 1
            return row * (self.n_band // 2) + band + south * (self.n_band - 1 - 2 * band)
        return row * self.n_band + band

    def fourier(self):
        n = np.arange(self.lon_cells)
        out = np.zeros((2, self.table_rows, self.lon_cells), np.float32)
        for g in range(self.groups):
            for i in range(GROUP):
                order = self.order(g, i, np.arange(self.stride[g]))
                live = order < self.degrees
                phase = (order[:, None] * n[None, :]) % self.lon_cells * (2.0 * np.pi / self.lon_cells)
                factor = np.where(order == 0, 1.0, np.sqrt(2.0)) * live / np.sqrt(self.lon_cells)
                at = slice(self.table_at[g] + i, self.table_at[g] + GROUP * self.stride[g], GROUP)
                out[0, at] = factor[:, None] * np.cos(phase)
                out[1, at] = -factor[:, None] * np.sin(phase)
        top = out.astype(ml_dtypes.bfloat16)
        low = (out - top.astype(np.float32)).astype(ml_dtypes.bfloat16)
        return top, low

    def seed_orders(self):
        device = np.arange(round_up(self.devices, LANES)) % self.devices
        row, band = device // self.n_band, device % self.n_band
        orders = [
            self.order(g, i, self.owner(g, row, band)) for g in range(self.groups) for i in range(GROUP)
        ]
        return np.minimum(np.stack(orders), self.degrees).astype(np.float32)

    def turn(self):
        at = np.arange(self.wide)
        back = at // self.lat_rows * self.lat_rows + (self.lat_rows - 1 - at % self.lat_rows)
        return np.stack([at[:, None] == at[None, :], at[:, None] == back[None, :]])

    def placement(self):
        turn = self.turn()
        width = max(b - a for a, b in self.span) * LANES
        out = np.zeros((2, 2, width, self.wide), bool)
        for p in range(2):
            start = p * self.wide - self.span[p][0] * LANES
            out[:, p, start : start + self.wide] = turn
        return out.astype(ml_dtypes.bfloat16)

    def latitudes(self):
        lane = np.arange(self.lat_lanes)
        inside = lane % LANES
        live = inside < self.per_block * self.lat_rows
        row = lane // LANES * (self.per_block * self.lat_rows) + np.where(live, inside, 0)
        angle = (row.astype(np.float32) + np.float32(0.5)) * np.float32(np.pi / self.lat_total)
        angle = angle.astype(np.float32).astype(np.float64)
        sine = np.sin(angle).astype(np.float32)
        quadrature = np.sqrt(sine * np.float32(np.pi / self.lat_total)) * live
        rows = np.zeros((8, self.lat_lanes), np.float32)
        rows[0] = np.cos(angle)
        rows[1] = np.log(sine.astype(np.float64))
        rows[2] = quadrature
        return rows


def route_observed(plan, orders_ref, observed_ref, routed_ref):
    slots = plan.groups * GROUP
    row, band = lax.axis_index("shell"), lax.axis_index("band")
    held = observed_ref.shape[0]
    lane = lax.broadcasted_iota(jnp.int32, (1, round_up(held, LANES)), 1)

    def read(t, orders):
        return jnp.where(lane == t, orders_ref[band * held + t], orders)

    orders = lax.fori_loop(0, held, read, jnp.full(lane.shape, plan.degrees, jnp.int32))
    orders = orders[:, :held]
    shape = (plan.n_band, GROUP, held)
    slot = lax.broadcasted_iota(jnp.int32, shape, 1)
    to_band = lax.broadcasted_iota(jnp.int32, shape, 0)
    if plan.halved:
        half_band = jnp.minimum(to_band, plan.n_band - 1 - to_band) + row * (plan.n_band // 2)
    wanted = []
    for g in range(plan.groups):
        owner = half_band if plan.is_half(g) else to_band + row * plan.n_band
        order = plan.order(g, slot, owner)
        wanted.append(jnp.where(order < plan.degrees, order, -1))
    wanted = jnp.concatenate(wanted, axis=1)
    chosen = jnp.where(wanted == orders[None], 1.0, 0.0).reshape(plan.n_band * slots, -1)
    chosen = chosen.astype(jnp.bfloat16)
    for p in range(2):
        top, low = split_parts(observed_ref[:, p, :])
        rows = (dot_ab(chosen, top) + dot_ab(chosen, low)).reshape(
            plan.n_band // 2, 2, slots, plan.degrees
        )
        for g in range(plan.groups):
            for t in range(plan.degree_tiles[g]):
                at = plan.seen_at[g] + (p * plan.degree_tiles[g] + t) * GROUP
                routed_ref[:, :, at : at + GROUP, :] = rows[
                    :, :, g * GROUP : (g + 1) * GROUP, t * LANES : (t + 1) * LANES
                ]


def place_fields(plan, south, density_ref, momentum_ref, place_ref, field_top, field_low):
    density = density_ref[...]
    ahead = (1.0 - 0.5 * STEP * STEP) * density + STEP * momentum_ref[...]
    top, low = split_parts(jnp.concatenate([density, ahead], axis=0))
    for p in range(2):
        place = place_ref[south, p]
        field_top[p] = dot_ab(place, top).astype(jnp.bfloat16)
        field_low[p] = dot_ab(place, low).astype(jnp.bfloat16)


def spectra(plan, group, field_top, field_low, top_ref, low_ref, ratio_ref, out_ref):
    parts = []
    for p in range(2):
        table_top = top_ref[p]
        parts.append(
            dot_abt(table_top, field_top[p]) + dot_abt(table_top, field_low[p])
            + dot_abt(low_ref[p], field_top[p])
        )
    tiles = []
    for t in range(plan.tiles):
        tile = None
        for p, (first, last) in enumerate(plan.span):
            if first <= t < last:
                piece = parts[p][:, (t - first) * LANES : (t - first + 1) * LANES]
                tile = piece if tile is None else tile + piece
        tiles.append(tile.reshape(-1, GROUP, LANES))
    row, owners = plan.row_at[group], plan.stride[group]
    for t in range(plan.tiles):
        out_ref[0:owners, row + t * GROUP : row + (t + 1) * GROUP, :] = tiles[t]
    if group == plan.groups - 1:
        for s in range(plan.local_shells):
            at = plan.ratio_row + s
            out_ref[0:owners, at : at + 1, :] = jnp.full((owners, 1, LANES), ratio_ref[s], jnp.float32)
        spare = plan.rows - plan.ratio_row - plan.local_shells
        if spare:
            out_ref[0:owners, plan.rows - spare :, :] = jnp.zeros((owners, spare, LANES), jnp.float32)


def add_grids(plan, group, recv_ref, top_ref, low_ref, total):
    row, owners = plan.row_at[group], plan.stride[group]
    tiles = []
    for t in range(plan.tiles):
        tile = recv_ref[0:owners, row + t * GROUP : row + (t + 1) * GROUP, :]
        tiles.append(tile.reshape(-1, LANES))
    for p, (first, last) in enumerate(plan.span):
        top, low = split_parts(jnp.concatenate(tiles[first:last], axis=1))
        table_top = top_ref[p]
        value = dot_atb(top, table_top) + dot_atb(low, table_top) + dot_atb(top, low_ref[p])
        start = p * plan.wide - first * LANES
        total[...] += value[start : start + plan.wide]


def legendre(plan, groups, me, owners, seed_ref, lat_ref, table_top, table_low):
    shape, full = (GROUP, LANES), (GROUP, plan.lat_lanes)
    slot = lax.broadcasted_iota(jnp.int32, shape, 0)
    lane = lax.broadcasted_iota(jnp.int32, shape, 1)
    cosine = jnp.broadcast_to(lat_ref[0:1, :], full)
    per_tile = LANES // RENORM
    growths, dampings, states = {}, {}, {}
    for group in groups:
        order = jnp.minimum(plan.order(group, slot, owners[group]), plan.degrees)
        order_value = order.astype(jnp.float32)
        for t in range(-(-plan.depth[group] // LANES)):
            step_int = lane + (t * LANES + 1)
            step = step_int.astype(jnp.float32)
            total = order_value + step
            growth = jnp.sqrt((4.0 * total * total - 1.0) / (step * (2.0 * order_value + step)))
            growth = jnp.where(order + step_int < plan.degrees, growth, 0.0)
            lower = (total - 1.0) * (total - 1.0)
            damping = jnp.sqrt(
                (step - 1.0) * (2.0 * order_value + step - 1.0) / jnp.maximum(4.0 * lower - 1.0, 1.0)
            )
            growths[group, t], dampings[group, t] = growth, growth * damping
        seed = seed_ref[group * GROUP : (group + 1) * GROUP, :]
        device = lax.broadcasted_iota(jnp.int32, seed.shape, 1)
        seed = jnp.sum(jnp.where(device == me, seed, 0.0), axis=1, keepdims=True)
        orders = order_value[:, 0:1]
        log_value = orders * lat_ref[1:2, :] + seed
        current = jnp.where(orders < plan.degrees, jnp.ones(full, jnp.float32), 0.0)
        states[group] = (current, jnp.zeros(full, jnp.float32), log_value)

    def one_span(t, active, i, carry):
        quadrature = jnp.broadcast_to(lat_ref[2:3, :], full)
        shift = lax.rem(LANES - i * RENORM, LANES)
        growth_tiles = [pltpu.roll(growths[group, t], shift, 1) for group in active]
        damping_tiles = [pltpu.roll(dampings[group, t], shift, 1) for group in active]
        factors = [jnp.exp(log_value) * quadrature for _, _, log_value in carry]
        now = [current for current, _, _ in carry]
        before = [previous for _, previous, _ in carry]
        values = [[[], []] for _ in active]
        for step in range(RENORM):
            for at, group in enumerate(active):
                parity = step % 2
                values[at][parity].append(now[at] * factors[at])
                growth = growth_tiles[at][:, step : step + 1]
                damping = damping_tiles[at][:, step : step + 1]
                following = (growth * cosine) * now[at] - damping * before[at]
                now[at], before[at] = following, now[at]
                if len(values[at][parity]) == 2:
                    row = plan.half_at[group] * GROUP + (t * per_tile + i) * (RENORM // 2 * GROUP)
                    row = pl.multiple_of(row + step // 4 * (2 * GROUP), 2 * GROUP)
                    top, low = split_parts(jnp.concatenate(values[at][parity], axis=0))
                    table_top[parity, pl.ds(row, 2 * GROUP), :] = top
                    table_low[parity, pl.ds(row, 2 * GROUP), :] = low
                    values[at][parity] = []
        out = []
        for at, (_, _, log_value) in enumerate(carry):
            largest = jnp.maximum(jnp.abs(now[at]), jnp.abs(before[at]))
            largest = jnp.where(largest == 0.0, 1.0, largest)
            inverse = 1.0 / largest
            out.append((now[at] * inverse, before[at] * inverse, log_value + jnp.log(largest)))
        return tuple(out)

    for t in range(-(-max(plan.depth[group] for group in groups) // LANES)):
        active = [group for group in groups if plan.depth[group] > t * LANES]
        count = min(min(per_tile, (plan.depth[group] - t * LANES) // RENORM) for group in active)
        carry = lax.fori_loop(0, count, functools.partial(one_span, t, active),
                              tuple(states[group] for group in active))
        for group, state in zip(active, carry):
            states[group] = state


def moved(tiles, start, width, dest):
    first, offset = start // LANES, start % LANES
    shift = (dest - offset) % LANES
    turn = lambda x: pltpu.roll(x, shift, 1) if shift else x
    value = turn(tiles[first])
    if offset + width > LANES:
        lane = lax.broadcasted_iota(jnp.int32, value.shape, 1)
        value = jnp.where(lane < dest + LANES - offset, value, turn(tiles[first + 1]))
    return value


def gather_fields(plan, group, sign, recv_ref, fold_top, fold_low):
    row, half_group = plan.row_at[group], plan.is_half(group)
    lane = lax.broadcasted_iota(jnp.int32, (GROUP, LANES), 1)
    width = plan.lat_rows
    for sy in range(plan.n_shell):
        for block in range(plan.blocks):
            sides = {}
            for inside in range(plan.per_block):
                band = block * plan.per_block + inside
                sources = [sy * plan.n_band + band, (sy + 1) * plan.n_band - 1 - band]
                if half_group:
                    sources = [sy * (plan.n_band // 2) + band]
                for side, source in enumerate(sources):
                    tiles = [
                        recv_ref[source, row + t * GROUP : row + (t + 1) * GROUP, :]
                        for t in range(plan.tiles)
                    ]
                    for piece in range(4 * plan.local_shells):
                        value = moved(tiles, piece * width, width, inside * width)
                        if inside:
                            value = jnp.where(lane < inside * width, sides[side, piece], value)
                        sides[side, piece] = value
            for field in range(2):
                for s in range(plan.local_shells):
                    pieces = [(p * 2 + field) * plan.local_shells + s for p in range(2)]
                    north = jnp.concatenate([sides[0, at] for at in pieces], axis=0)
                    if half_group:
                        folds = (north, sign * north)
                    else:
                        south = jnp.concatenate([sides[1, at] for at in pieces], axis=0)
                        folds = (north + south, north - south)
                    start = field * plan.columns + (sy * plan.local_shells + s) * 2 * GROUP
                    for parity, folded in enumerate(folds):
                        top, low = split_parts(folded)
                        at = (parity, pl.ds(start, 2 * GROUP), pl.ds(block * LANES, LANES))
                        fold_top[at] = top
                        fold_low[at] = low


def scatter_fields(plan, group, grids, send_ref):
    row, width = plan.row_at[group], plan.lat_rows
    lane = lax.broadcasted_iota(jnp.int32, (GROUP, LANES), 1)
    bands = plan.n_band // 2 if plan.is_half(group) else plan.n_band
    for sy in range(plan.n_shell):
        for band in range(bands):
            side = int(band >= plan.n_band // 2)
            mirrored = plan.n_band - 1 - band if side else band
            block, inside = mirrored // plan.per_block, mirrored % plan.per_block
            tiles = []
            for t in range(plan.tiles):
                tile = None
                for piece in range(4 * plan.local_shells):
                    start = piece * width - t * LANES
                    if start + width <= 0 or start >= LANES:
                        continue
                    p, field, s = piece // (2 * plan.local_shells), piece // plan.local_shells % 2, piece % plan.local_shells
                    at = ((sy * plan.local_shells + s) * 2 + p) * GROUP
                    value = grids[field][side][at : at + GROUP, pl.ds(block * LANES, LANES)]
                    shift = (start - inside * width) % LANES
                    if shift:
                        value = pltpu.roll(value, shift, 1)
                    tile = value if tile is None else jnp.where(lane < start, tile, value)
                tiles.append(tile)
            for t in range(plan.tiles):
                send_ref[sy * bands + band, row + t * GROUP : row + (t + 1) * GROUP, :] = tiles[t]


def degree_lanes(plan, group, owner, precision_ref, total, weight_ref, seen_ref):
    width = round_up(plan.groups * GROUP * plan.devices + plan.degrees, LANES)
    row = jnp.concatenate(
        [precision_ref[...].reshape(1, plan.degrees), jnp.zeros((1, width - plan.degrees), jnp.float32)], axis=1
    )
    row = jnp.broadcast_to(row, (GROUP, width))
    sub = lax.broadcasted_iota(jnp.int32, (GROUP, width), 0)
    precision = row
    for i in range(GROUP):
        start = plan.order(group, i, 0)
        precision = jnp.where(sub == i, pltpu.roll(row, (width - start) % width, 1), precision)
    precision = pltpu.roll(precision, lax.rem(width - owner, width), 1)
    copies = plan.columns // GROUP
    nothing = jnp.zeros((plan.columns - 2 * GROUP, LANES), jnp.float32)
    for t in range(plan.degree_tiles[group]):
        rows = pl.ds(plan.degree_at[group] + t * LANES, LANES)
        tile = precision[:, t * LANES : (t + 1) * LANES]
        weight_ref[rows, :] = jnp.concatenate([tile] * copies, axis=0).T
        tiles = []
        for p in range(2):
            at = plan.seen_at[group] + (p * plan.degree_tiles[group] + t) * GROUP
            tiles.append(total[at : at + GROUP, :])
        seen_ref[rows, :] = jnp.concatenate(tiles + [nothing], axis=0).T


class Misfit:
    def __init__(self, plan, group, owner, sign, log_ratio, seen_ref, weight_ref, table_top, table_low,
                 fold_top, fold_low):
        self.plan, self.group, self.sign, self.log_ratio = plan, group, sign, log_ratio
        self.seen_ref, self.weight_ref = seen_ref, weight_ref
        self.table_top, self.table_low = table_top, table_low
        self.fold_top, self.fold_low = fold_top, fold_low
        columns = self.columns = plan.columns
        half_depth = plan.depth[group] // 2
        chunk = max(c for c in range(RENORM // 2, 65, RENORM // 2) if half_depth % c == 0)
        self.chunk, self.chunks = chunk, half_depth // chunk
        self.lane = lax.broadcasted_iota(jnp.int32, (chunk, columns), 1)
        order = plan.order(group, lax.rem(self.lane, GROUP), owner)
        imaginary = lax.rem(self.lane // GROUP, 2) == 1
        self.keep = jnp.where((order == 0) & imaginary, 0.0, 1.0)
        self.offset = lax.broadcasted_iota(jnp.int32, (chunk, columns), 0) * 2 + order
        own_row = lax.broadcasted_iota(jnp.int32, (GROUP, columns), 0)
        own_lane = lax.rem(lax.broadcasted_iota(jnp.int32, (GROUP, columns), 1), GROUP)
        self.own = jnp.where(own_row == own_lane, 1.0, 0.0)

    def over_shells(self, x):
        shift = 2 * GROUP
        while shift < self.columns:
            x = x + pltpu.roll(x, shift, 1)
            shift *= 2
        return x

    def rows_at(self, c):
        size = self.chunk * GROUP
        start = self.plan.half_at[self.group] * GROUP + c * size
        return pl.ds(pl.multiple_of(start, size), size)

    def pick(self, values):
        return jnp.sum(values.reshape(self.chunk, GROUP, self.columns) * self.own[None], axis=1)

    def degrees_at(self, c, parity):
        start = self.plan.degree_at[self.group] + c * (2 * self.chunk) + parity
        return pl.ds(start, self.chunk, stride=2)

    def radial_at(self, c, parity):
        degree = self.offset + (c * (2 * self.chunk) + parity)
        return jnp.exp(degree.astype(jnp.float32) * self.log_ratio)

    def seen_at(self, c, parity):
        return self.seen_ref[self.degrees_at(c, parity), :]

    def weight_at(self, c, parity):
        return self.weight_ref[self.degrees_at(c, parity), :]

    def terms_of_both(self, c, parity):
        rows = self.rows_at(c)
        top = self.table_top[parity, rows, :]
        terms = (dot_abt(top, self.fold_top[parity]) + dot_abt(top, self.fold_low[parity])
                 + dot_abt(self.table_low[parity, rows, :], self.fold_top[parity]))
        return terms[:, : self.columns], terms[:, self.columns :]

    def fold_again(self, parity, folded):
        top, low = split_parts(folded)
        self.fold_top[parity, 0 : self.columns, :] = top
        self.fold_top[parity, self.columns : 2 * self.columns, :] = low

    def terms_again(self, c, parity):
        rows = self.rows_at(c)
        both = dot_abt(self.table_top[parity, rows, :], self.fold_top[parity])
        return (both[:, : self.columns] + both[:, self.columns :]
                + dot_abt(self.table_low[parity, rows, :], self.fold_top[parity, 0 : self.columns, :]))

    def adjoint(self, c, parity, weighted):
        rows = self.rows_at(c)
        wide = weighted[:, None, :] * self.own[None]
        top, low = split_parts(wide.reshape(self.chunk * GROUP, self.columns))
        both = dot_atb(jnp.concatenate([top, low], axis=1), self.table_top[parity, rows, :])
        return (both[: self.columns] + both[self.columns :]
                + dot_atb(top, self.table_low[parity, rows, :]))


def misfit_group(work, recv_ref, wanted_ref, grid_ref, send_ref):
    plan, group, chunk = work.plan, work.group, work.chunk
    gather_fields(plan, group, work.sign, recv_ref, work.fold_top, work.fold_low)

    def first_pass(c, carry):
        tall = pl.ds(pl.multiple_of(c * chunk, chunk), chunk)
        terms = [work.terms_of_both(c, parity) for parity in range(2)]
        for parity in range(2):
            radial, seen = work.radial_at(c, parity), work.seen_at(c, parity)
            first, ahead = (
                work.over_shells(work.pick(values) * radial - seen) for values in terms[parity]
            )
            wanted_ref[parity, tall, :] = ahead
            grid_ref[0, parity] += work.adjoint(c, parity, radial * work.weight_at(c, parity) * first)
        return carry

    def second_pass(c, carry):
        tall = pl.ds(pl.multiple_of(c * chunk, chunk), chunk)
        terms = [work.terms_again(c, parity) for parity in range(2)]
        for parity in range(2):
            radial = work.radial_at(c, parity)
            back = work.over_shells(work.pick(terms[parity]) * radial) * work.keep
            misfit = wanted_ref[parity, tall, :] - (0.5 * STEP * STEP) * back
            grid_ref[1, parity] += work.adjoint(c, parity, radial * work.weight_at(c, parity) * misfit)
        return carry

    grid_ref[...] = jnp.zeros_like(grid_ref)
    lax.fori_loop(0, work.chunks, first_pass, 0)
    for parity in range(2):
        work.fold_again(parity, 2.0 * grid_ref[0, parity])
    lax.fori_loop(0, work.chunks, second_pass, 0)

    for field in range(2):
        even, odd = grid_ref[field, 0], grid_ref[field, 1]
        grid_ref[field, 0] = even + odd
        grid_ref[field, 1] = even - odd
    grids = [[grid_ref.at[field, side] for side in range(2)] for field in range(2)]
    scatter_fields(plan, group, grids, send_ref)


def pack(work, values):
    packed = values[:GROUP]
    for block in range(1, work.chunk // GROUP):
        rows = values[block * GROUP : (block + 1) * GROUP]
        packed = jnp.where(work.lane[:GROUP] // (2 * GROUP) == block, rows, packed)
    return packed


def unpack(work, packed):
    blocks = []
    for block in range(work.chunk // GROUP):
        inside = work.lane[:GROUP] // (2 * GROUP) == block
        blocks.append(work.over_shells(jnp.where(inside, packed, 0.0)))
    return jnp.concatenate(blocks, axis=0)


def half_first(work, recv_ref, part_ref, swap_ref):
    gather_fields(work.plan, work.group, work.sign, recv_ref, work.fold_top, work.fold_low)
    for parity in range(2):
        radial = work.radial_at(0, parity)
        for field, values in enumerate(work.terms_of_both(0, parity)):
            part = work.over_shells(work.pick(values) * radial)
            at = 2 * field + parity
            part_ref[at] = part
            swap_ref[at * GROUP : (at + 1) * GROUP, :] = pack(work, part)


def half_second(work, part_ref, grid_ref, swap_ref, came_ref):
    grids = []
    for parity in range(2):
        seen = work.over_shells(work.seen_at(0, parity))
        first, ahead = (
            part_ref[at] + unpack(work, came_ref[at * GROUP : (at + 1) * GROUP, :]) - seen
            for at in (parity, 2 + parity)
        )
        part_ref[2 + parity] = ahead
        weighted = work.radial_at(0, parity) * work.weight_at(0, parity) * first
        grids.append(work.adjoint(0, parity, weighted))
    grid = grids[0] + work.sign * grids[1]
    grid_ref[0] = grid
    work.fold_again(0, grid)
    work.fold_again(1, work.sign * grid)
    for parity in range(2):
        part = work.over_shells(work.pick(work.terms_again(0, parity)) * work.radial_at(0, parity))
        part_ref[parity] = part
        swap_ref[parity * GROUP : (parity + 1) * GROUP, :] = pack(work, part)


def half_third(work, part_ref, grid_ref, came_ref, send_ref):
    grids = []
    for parity in range(2):
        back = part_ref[parity] + unpack(work, came_ref[parity * GROUP : (parity + 1) * GROUP, :])
        misfit = part_ref[2 + parity] - (0.5 * STEP * STEP) * back
        weighted = work.radial_at(0, parity) * work.weight_at(0, parity) * misfit
        grids.append(work.adjoint(0, parity, weighted))
    grid_ref[1] = grids[0] + work.sign * grids[1]
    scatter_fields(work.plan, work.group, [[grid_ref.at[0]], [grid_ref.at[1]]], send_ref)


def step_kernel(plan, density_ref, momentum_ref, place_ref, observed_ref, precision_ref,
                seed_ref, lat_ref, orders_ref, ratio_ref, top_hbm, low_hbm, total_ref, fourier_top,
                fourier_low, field_top, field_low, sent_ref, recv_ref, back_ref, out_ref,
                routed_ref, pair_ref, owned_ref, table_top, table_low, fold_top, fold_low, wanted_ref,
                grid_ref, weight_ref, seen_ref, part_ref, half_grid_ref, swap_ref, came_ref, load_sems,
                send_sem, recv_sem, back_send_sem, back_recv_sem, pair_sems, owned_sems, swap_sems):
    n, n_band = plan.devices, plan.n_band
    row, band = lax.axis_index("shell"), lax.axis_index("band")
    me = row * n_band + band
    south = (band >= n_band // 2).astype(jnp.int32)
    barrier = pltpu.get_barrier_semaphore()

    def peer(i):
        to = lax.rem(me + i, n)
        return to, (to // n_band, lax.rem(to, n_band))

    def greet(i, carry):
        pl.semaphore_signal(barrier, inc=1, device_id=peer(i)[1], device_id_type=MESH)
        return carry

    def rows_of(group):
        end = plan.row_at[group + 1] if group + 1 < plan.groups else plan.rows
        return pl.ds(plan.row_at[group], end - plan.row_at[group])

    owners = [me] * plan.groups
    if plan.halved:
        owners[-1] = row * (n_band // 2) + band + south * (n_band - 1 - 2 * band)

    def start_group(group, source, target, sent_sems, got_sems):
        rows, mine, count = rows_of(group), owners[group], plan.stride[group]
        bands = count // plan.n_shell
        turned = south if plan.is_half(group) else 0
        pltpu.make_async_copy(
            source.at[mine, rows], target.at[mine, rows], got_sems.at[group]
        ).start()

        def send(i, carry):
            to = lax.rem(mine + i, count)
            pltpu.make_async_remote_copy(
                src_ref=source.at[to, rows], dst_ref=target.at[mine, rows],
                send_sem=sent_sems.at[group], recv_sem=got_sems.at[group],
                device_id=(to // bands, turned * (n_band - 1) + (1 - 2 * turned) * lax.rem(to, bands)),
                device_id_type=MESH,
            ).start()
            return carry

        lax.fori_loop(1, count, send, 0)

    def wait_for(ref, sem):
        pltpu.make_async_copy(ref, ref, sem).wait()

    def load(group, part):
        source, target = ((top_hbm, fourier_top), (low_hbm, fourier_low))[part]
        rows = pl.ds(plan.table_at[group], GROUP * plan.stride[group])
        return pltpu.make_async_copy(source.at[:, rows], target.at[:, rows], load_sems.at[group, part])

    def fourier(group):
        rows = pl.ds(plan.table_at[group], GROUP * plan.stride[group])
        return fourier_top.at[:, rows], fourier_low.at[:, rows]

    for group in plan.turns:
        for part in range(2):
            load(group, part).start()
    lax.fori_loop(1, n, greet, 0)
    place_fields(plan, south, density_ref, momentum_ref, place_ref, field_top, field_low)

    core, place, places = lax.rem(band, 2), band // 2, n_band // 2
    pair_copy = pltpu.make_async_remote_copy(
        src_ref=routed_ref.at[:, 1 - core], dst_ref=pair_ref, send_sem=pair_sems.at[0],
        recv_sem=pair_sems.at[1], device_id=(row, band + 1 - 2 * core), device_id_type=MESH,
    )

    def hand_over(i, carry):
        to = lax.rem(place + i, places)
        pltpu.make_async_remote_copy(
            src_ref=pair_ref.at[to], dst_ref=owned_ref.at[place], send_sem=owned_sems.at[0],
            recv_sem=owned_sems.at[1], device_id=(row, 2 * to + core), device_id_type=MESH,
        ).start()
        return carry

    def share_observed():
        pair_copy.wait()
        pair_ref[...] += routed_ref[:, core]
        pltpu.make_async_copy(pair_ref.at[place], owned_ref.at[place], owned_sems.at[1]).start()
        lax.fori_loop(1, places, hand_over, 0)

    def rows_made(*groups):
        legendre(plan, groups, me, owners, seed_ref, lat_ref, table_top, table_low)

    def arrived(group):
        count = pl.ds(0, plan.stride[group])
        wait_for(recv_ref.at[count, rows_of(group)], recv_sem.at[group])

    sign = jnp.where(south == 1, -1.0, 1.0)
    last = plan.turns[0]
    full = plan.turns[1:] if plan.halved else plan.turns

    def log_ratios():
        lane = lax.broadcasted_iota(jnp.int32, (1, plan.columns), 1)
        ratio = jnp.ones((1, plan.columns), jnp.float32)
        for sy in range(plan.n_shell):
            for s in range(plan.local_shells):
                at = plan.ratio_row + s
                value = recv_ref[sy * (plan.stride[last] // plan.n_shell), at : at + 1, :]
                ratio = jnp.where(lane // (2 * GROUP) == sy * plan.local_shells + s, value, ratio)
        return jnp.log(ratio)

    def work_on(group):
        return Misfit(plan, group, owners[group], sign, log_ratio, seen_ref, weight_ref, table_top,
                      table_low, fold_top, fold_low)

    def swap(turn):
        count = (4, 2)[turn] * GROUP
        return pltpu.make_async_remote_copy(
            src_ref=swap_ref.at[turn, pl.ds(0, count)], dst_ref=came_ref.at[turn, pl.ds(0, count)],
            send_sem=swap_sems.at[turn, 0], recv_sem=swap_sems.at[turn, 1],
            device_id=(row, n_band - 1 - band), device_id_type=MESH,
        )

    for turn, group in enumerate(plan.turns):
        for part in range(2):
            load(group, part).wait()
        spectra(plan, group, field_top, field_low, *fourier(group), ratio_ref, sent_ref)
        if turn == 0:
            pl.semaphore_wait(barrier, n - 1)
        start_group(group, sent_ref, recv_ref, send_sem, recv_sem)
        if turn == 0:
            route_observed(plan, orders_ref, observed_ref, routed_ref)
            pair_copy.start()
        if turn == min(1, plan.groups - 1):
            share_observed()
            rows_made(last)
            arrived(last)
            log_ratio = log_ratios()
            if plan.halved:
                half = work_on(last)
                half_first(half, recv_ref, part_ref, swap_ref.at[0])
                swap(0).start()

    if plan.groups > 1:
        rows_made(*plan.turns[1:])
    wait_for(owned_ref, owned_sems.at[1])
    owned = owned_ref[0]
    for z in range(1, places):
        owned = owned + owned_ref[z]
    owned_ref[0] = owned
    for group in range(plan.groups):
        degree_lanes(plan, group, owners[group], precision_ref, owned_ref.at[0], weight_ref, seen_ref)

    for group in full:
        if group != last:
            arrived(group)
        misfit_group(work_on(group), recv_ref, wanted_ref, grid_ref, back_ref)
        start_group(group, back_ref, out_ref, back_send_sem, back_recv_sem)
        if plan.halved and group == full[0]:
            swap(0).wait()
            half_second(half, part_ref, half_grid_ref, swap_ref.at[1], came_ref.at[0])
            swap(1).start()
    if plan.halved:
        swap(1).wait()
        half_third(half, part_ref, half_grid_ref, came_ref.at[1], back_ref)
        start_group(last, back_ref, out_ref, back_send_sem, back_recv_sem)

    total_ref[...] = jnp.zeros_like(total_ref)
    for group in full[:-1] + ([last] if plan.halved else []) + full[-1:]:
        count = pl.ds(0, plan.stride[group])
        wait_for(out_ref.at[count, rows_of(group)], back_recv_sem.at[group])
        add_grids(plan, group, out_ref, *fourier(group), total_ref)
    for group in range(plan.groups):
        rows, count = rows_of(group), pl.ds(0, plan.stride[group] - 1)
        wait_for(sent_ref.at[count, rows], send_sem.at[group])
        wait_for(back_ref.at[count, rows], back_send_sem.at[group])
    if places > 1:
        wait_for(pair_ref.at[pl.ds(0, places - 1)], owned_sems.at[0])


def step(plan, density, momentum, observed, precision, seed, orders, ratio):
    vmem = pl.BlockSpec(memory_space=pltpu.VMEM)
    smem = pl.BlockSpec(memory_space=pltpu.SMEM)
    hbm = pl.BlockSpec(memory_space=pl.ANY)
    fourier = [jnp.asarray(x) for x in plan.fourier()]
    placement = jnp.asarray(plan.placement())
    f32, bf16 = jnp.float32, jnp.bfloat16
    field = pltpu.VMEM((2, placement.shape[2], plan.lon_cells), bf16)
    chunks = pltpu.VMEM((plan.devices, plan.rows, LANES), f32)
    routed = pltpu.VMEM((plan.n_band // 2, 2, plan.seen_rows, LANES), f32)
    owned = pltpu.VMEM((plan.n_band // 2, plan.seen_rows, LANES), f32)
    table = pltpu.VMEM((2, plan.half_all * GROUP, plan.lat_lanes), bf16)
    fold = pltpu.VMEM((2, 2 * plan.columns, plan.lat_lanes), bf16)
    by_degree = pltpu.VMEM((plan.degree_all, plan.columns), f32)
    swap = pltpu.VMEM((2, 4 * GROUP, plan.columns), f32)
    sems = lambda *count: pltpu.SemaphoreType.DMA(count)
    return pl.pallas_call(
        functools.partial(step_kernel, plan),
        out_shape=jax.ShapeDtypeStruct((plan.wide, plan.lon_cells), f32),
        in_specs=[vmem] * 7 + [smem] * 2 + [hbm] * 2,
        out_specs=vmem,
        scratch_shapes=[pltpu.VMEM(fourier[0].shape, bf16)] * 2
        + [field] * 2 + [chunks] * 4
        + [routed, owned, owned, table, table, fold, fold,
           pltpu.VMEM((2, plan.depth[0] // 2, plan.columns), f32),
           pltpu.VMEM((2, 2, plan.columns, plan.lat_lanes), f32), by_degree, by_degree,
           pltpu.VMEM((4, plan.depth[-1] // 2, plan.columns), f32),
           pltpu.VMEM((2, plan.columns, plan.lat_lanes), f32), swap, swap]
        + [sems(plan.groups, 2)] + [sems(plan.groups)] * 4 + [sems(2)] * 2 + [sems(2, 2)],
        compiler_params=pltpu.CompilerParams(
            collective_id=0, has_side_effects=True, vmem_limit_bytes=VMEM_LIMIT
        ),
        name="step",
    )(density, momentum, placement, observed, precision, seed, jnp.asarray(plan.latitudes()),
      orders, ratio, *fourier)


def finish_kernel(plan, total_ref, turn_ref, density_ref, momentum_ref, new_density_ref, new_momentum_ref):
    south = (lax.axis_index("band") >= plan.n_band // 2).astype(jnp.int32)
    top, low = split_parts(total_ref[...])
    turn = turn_ref[south]
    grid = dot_ab(turn, top) + dot_ab(turn, low)
    density, momentum = density_ref[...], momentum_ref[...]
    half_momentum = momentum - 0.5 * STEP * (density + grid[: plan.cells])
    new_density = density + STEP * half_momentum
    new_density_ref[...] = new_density
    new_momentum_ref[...] = half_momentum - 0.5 * STEP * (new_density + grid[plan.cells :])


def finish(plan, total, density, momentum):
    turn = jnp.asarray(plan.turn().astype(ml_dtypes.bfloat16))
    wide = 2 * LANES if plan.lon_cells % (2 * LANES) == 0 else plan.lon_cells
    at_lanes = lambda rows: pl.BlockSpec((rows, wide), lambda i: (0, i))
    shape = jax.ShapeDtypeStruct(density.shape, jnp.float32)
    return pl.pallas_call(
        functools.partial(finish_kernel, plan),
        grid=(plan.lon_cells // wide,),
        in_specs=[at_lanes(plan.wide), pl.BlockSpec(turn.shape, lambda i: (0, 0, 0)),
                  at_lanes(plan.cells), at_lanes(plan.cells)],
        out_specs=[at_lanes(plan.cells)] * 2,
        out_shape=[shape, shape],
        name="finish",
    )(total, turn, density, momentum)


def body(density, momentum, observed, order_list, shell_ratio, precision):
    slots, _, degrees = observed.shape
    local_shells, lat_rows, lon_cells = density.shape
    n_shell, n_band = lax.axis_size("shell"), lax.axis_size("band")
    plan = Plan(n_shell, n_band, local_shells, lat_rows, lon_cells, degrees)
    order_value = jnp.asarray(plan.seed_orders())
    seed = 0.5 * (
        jnp.log(order_value + 0.5)
        + lax.lgamma(2.0 * order_value + 1.0)
        - order_value * jnp.log(4.0)
        - 2.0 * lax.lgamma(order_value + 1.0)
    )
    flat_density = density.reshape(plan.cells, lon_cells)
    flat_momentum = momentum.reshape(plan.cells, lon_cells)
    total = step(plan, flat_density, flat_momentum, observed, precision, seed, order_list, shell_ratio)
    new_density, new_momentum = finish(plan, total, flat_density, flat_momentum)
    return new_density.reshape(density.shape), new_momentum.reshape(density.shape)


def solution(mesh):
    in_specs = (
        P("shell", "band", None),
        P("shell", "band", None),
        P("band", None, None),
        P(),
        P("shell"),
        P(),
    )
    out_specs = (P("shell", "band", None), P("shell", "band", None))
    return jax.shard_map(body, mesh=mesh, in_specs=in_specs, out_specs=out_specs, check_vma=False)
```

```python
import functools

import jax
import jax.numpy as jnp
import ml_dtypes
import numpy as np
from jax import lax
from jax.experimental import pallas as pl
from jax.experimental.pallas import tpu as pltpu
from jax.sharding import PartitionSpec as P

STEP = 0.5
LANES = 128
GROUP = 8
RENORM = 16
MESH = pl.DeviceIdType.MESH
VMEM_LIMIT = 58 * 1024 * 1024


def dot_ab(a, b):
    return lax.dot_general(a, b, (((1,), (0,)), ((), ())), preferred_element_type=jnp.float32)


def dot_abt(a, b):
    return lax.dot_general(a, b, (((1,), (1,)), ((), ())), preferred_element_type=jnp.float32)


def dot_atb(a, b):
    return lax.dot_general(a, b, (((0,), (0,)), ((), ())), preferred_element_type=jnp.float32)


def split_parts(x):
    top = x.astype(jnp.bfloat16)
    return top, (x - top.astype(jnp.float32)).astype(jnp.bfloat16)


def round_up(x, to):
    return -(-x // to) * to


class Plan:
    def __init__(self, n_shell, n_band, local_shells, lat_rows, lon_cells, degrees):
        self.n_shell, self.n_band, self.local_shells = n_shell, n_band, local_shells
        self.lat_rows, self.lon_cells, self.degrees = lat_rows, lon_cells, degrees
        self.devices = n_shell * n_band
        self.shells = n_shell * local_shells
        self.lat_total = n_band * lat_rows
        self.cells = local_shells * lat_rows
        full = degrees // (GROUP * self.devices)
        rest = degrees - full * GROUP * self.devices
        self.groups = full + (rest > 0)
        self.halved = full > 0 and 0 < rest <= min(GROUP * self.devices // 2, 2 * LANES // 2)
        self.half_devices = self.devices // 2
        self.base = [g * GROUP * self.devices for g in range(self.groups)]
        self.stride = [self.devices] * self.groups
        if self.halved:
            self.stride[-1] = self.half_devices
        self.table_at = [GROUP * sum(self.stride[:g]) for g in range(self.groups)]
        self.table_rows = GROUP * sum(self.stride)
        self.wide = 2 * self.cells
        self.tiles = -(-2 * self.wide // LANES)
        self.span = [
            (p * self.wide // LANES, -(-(p + 1) * self.wide // LANES)) for p in range(2)
        ]
        self.turns = [self.groups - 1] + list(range(self.groups - 1))
        self.sends = self.turns[1:2] + self.turns[:1] + self.turns[2:] if self.halved else self.turns
        self.row_at, rows = [], 0
        for g in range(self.groups):
            self.row_at.append(rows)
            used = self.tiles * GROUP
            if g == self.groups - 1:
                self.ratio_row = rows + used
                used += local_shells
            rows += round_up(used, 8)
        self.rows = rows
        self.depth = [
            min(degrees, round_up(degrees - base, 2 * RENORM)) for base in self.base
        ]
        self.half_at = [sum(self.depth[:g]) // 2 for g in range(self.groups)]
        self.half_all = sum(self.depth) // 2
        pairs = n_band // 2
        self.per_block = max(q for q in range(1, pairs + 1) if pairs % q == 0 and q * lat_rows <= LANES)
        self.blocks = pairs // self.per_block
        self.lat_lanes = self.blocks * LANES
        self.columns = 2 * GROUP * self.shells
        self.degree_tiles = [round_up(depth, LANES) // LANES for depth in self.depth]
        self.degree_at = [sum(self.degree_tiles[:g]) * LANES for g in range(self.groups)]
        self.degree_all = sum(self.degree_tiles) * LANES
        self.seen_at = [2 * GROUP * sum(self.degree_tiles[:g]) for g in range(self.groups)]
        self.seen_rows = 2 * GROUP * sum(self.degree_tiles)

    def is_half(self, g):
        return self.halved and g == self.groups - 1

    def order(self, g, slot, owner):
        return self.base[g] + slot * self.stride[g] + owner

    def owner(self, g, row, band):
        if self.is_half(g):
            south = (band >= self.n_band // 2) * 1
            return row * (self.n_band // 2) + band + south * (self.n_band - 1 - 2 * band)
        return row * self.n_band + band

    def fourier(self):
        n = np.arange(self.lon_cells)
        out = np.zeros((2, self.table_rows, self.lon_cells), np.float32)
        for g in range(self.groups):
            for i in range(GROUP):
                order = self.order(g, i, np.arange(self.stride[g]))
                live = order < self.degrees
                phase = (order[:, None] * n[None, :]) % self.lon_cells * (2.0 * np.pi / self.lon_cells)
                factor = np.where(order == 0, 1.0, np.sqrt(2.0)) * live / np.sqrt(self.lon_cells)
                at = slice(self.table_at[g] + i, self.table_at[g] + GROUP * self.stride[g], GROUP)
                out[0, at] = factor[:, None] * np.cos(phase)
                out[1, at] = -factor[:, None] * np.sin(phase)
        top = out.astype(ml_dtypes.bfloat16)
        low = (out - top.astype(np.float32)).astype(ml_dtypes.bfloat16)
        return top, low

    def seed_orders(self):
        device = np.arange(round_up(self.devices, LANES)) % self.devices
        row, band = device // self.n_band, device % self.n_band
        orders = [
            self.order(g, i, self.owner(g, row, band)) for g in range(self.groups) for i in range(GROUP)
        ]
        return np.minimum(np.stack(orders), self.degrees).astype(np.float32)

    def turn(self):
        at = np.arange(self.wide)
        back = at // self.lat_rows * self.lat_rows + (self.lat_rows - 1 - at % self.lat_rows)
        return np.stack([at[:, None] == at[None, :], at[:, None] == back[None, :]])

    def placement(self):
        turn = self.turn()
        width = max(b - a for a, b in self.span) * LANES
        out = np.zeros((2, 2, width, self.wide), bool)
        for p in range(2):
            start = p * self.wide - self.span[p][0] * LANES
            out[:, p, start : start + self.wide] = turn
        return out.astype(ml_dtypes.bfloat16)

    def latitudes(self):
        lane = np.arange(self.lat_lanes)
        inside = lane % LANES
        live = inside < self.per_block * self.lat_rows
        row = lane // LANES * (self.per_block * self.lat_rows) + np.where(live, inside, 0)
        angle = (row.astype(np.float32) + np.float32(0.5)) * np.float32(np.pi / self.lat_total)
        angle = angle.astype(np.float32).astype(np.float64)
        sine = np.sin(angle).astype(np.float32)
        quadrature = np.sqrt(sine * np.float32(np.pi / self.lat_total)) * live
        rows = np.zeros((8, self.lat_lanes), np.float32)
        rows[0] = np.cos(angle)
        rows[1] = np.log(sine.astype(np.float64))
        rows[2] = quadrature
        return rows


def route_observed(plan, orders_ref, observed_ref, routed_ref):
    slots = plan.groups * GROUP
    row, band = lax.axis_index("shell"), lax.axis_index("band")
    held = observed_ref.shape[0]
    lane = lax.broadcasted_iota(jnp.int32, (1, round_up(held, LANES)), 1)

    def read(t, orders):
        return jnp.where(lane == t, orders_ref[band * held + t], orders)

    orders = lax.fori_loop(0, held, read, jnp.full(lane.shape, plan.degrees, jnp.int32))
    orders = orders[:, :held]
    shape = (plan.n_band, GROUP, held)
    slot = lax.broadcasted_iota(jnp.int32, shape, 1)
    to_band = lax.broadcasted_iota(jnp.int32, shape, 0)
    if plan.halved:
        half_band = jnp.minimum(to_band, plan.n_band - 1 - to_band) + row * (plan.n_band // 2)
    wanted = []
    for g in range(plan.groups):
        owner = half_band if plan.is_half(g) else to_band + row * plan.n_band
        order = plan.order(g, slot, owner)
        wanted.append(jnp.where(order < plan.degrees, order, -1))
    wanted = jnp.concatenate(wanted, axis=1)
    chosen = jnp.where(wanted == orders[None], 1.0, 0.0).reshape(plan.n_band * slots, -1)
    chosen = chosen.astype(jnp.bfloat16)
    for p in range(2):
        top, low = split_parts(observed_ref[:, p, :])
        rows = (dot_ab(chosen, top) + dot_ab(chosen, low)).reshape(
            plan.n_band // 2, 2, slots, plan.degrees
        )
        for g in range(plan.groups):
            for t in range(plan.degree_tiles[g]):
                at = plan.seen_at[g] + (p * plan.degree_tiles[g] + t) * GROUP
                routed_ref[:, :, at : at + GROUP, :] = rows[
                    :, :, g * GROUP : (g + 1) * GROUP, t * LANES : (t + 1) * LANES
                ]


def place_fields(plan, south, density_ref, momentum_ref, place_ref, field_top, field_low):
    density = density_ref[...]
    ahead = (1.0 - 0.5 * STEP * STEP) * density + STEP * momentum_ref[...]
    top, low = split_parts(jnp.concatenate([density, ahead], axis=0))
    for p in range(2):
        place = place_ref[south, p]
        field_top[p] = dot_ab(place, top).astype(jnp.bfloat16)
        field_low[p] = dot_ab(place, low).astype(jnp.bfloat16)


def spectra(plan, group, field_top, field_low, top_ref, low_ref, ratio_ref, out_ref):
    parts = []
    for p in range(2):
        table_top = top_ref[p]
        parts.append(
            dot_abt(table_top, field_top[p]) + dot_abt(table_top, field_low[p])
            + dot_abt(low_ref[p], field_top[p])
        )
    tiles = []
    for t in range(plan.tiles):
        tile = None
        for p, (first, last) in enumerate(plan.span):
            if first <= t < last:
                piece = parts[p][:, (t - first) * LANES : (t - first + 1) * LANES]
                tile = piece if tile is None else tile + piece
        tiles.append(tile.reshape(-1, GROUP, LANES))
    row, owners = plan.row_at[group], plan.stride[group]
    for t in range(plan.tiles):
        out_ref[0:owners, row + t * GROUP : row + (t + 1) * GROUP, :] = tiles[t]
    if group == plan.groups - 1:
        for s in range(plan.local_shells):
            at = plan.ratio_row + s
            out_ref[0:owners, at : at + 1, :] = jnp.full((owners, 1, LANES), ratio_ref[s], jnp.float32)
        spare = plan.rows - plan.ratio_row - plan.local_shells
        if spare:
            out_ref[0:owners, plan.rows - spare :, :] = jnp.zeros((owners, spare, LANES), jnp.float32)


def add_grids(plan, group, recv_ref, top_ref, low_ref, total):
    row, owners = plan.row_at[group], plan.stride[group]
    tiles = []
    for t in range(plan.tiles):
        tile = recv_ref[0:owners, row + t * GROUP : row + (t + 1) * GROUP, :]
        tiles.append(tile.reshape(-1, LANES))
    for p, (first, last) in enumerate(plan.span):
        top, low = split_parts(jnp.concatenate(tiles[first:last], axis=1))
        table_top = top_ref[p]
        value = dot_atb(top, table_top) + dot_atb(low, table_top) + dot_atb(top, low_ref[p])
        start = p * plan.wide - first * LANES
        total[...] += value[start : start + plan.wide]


def legendre(plan, groups, me, owners, seed_ref, lat_ref, table_top, table_low):
    shape, full = (GROUP, LANES), (GROUP, plan.lat_lanes)
    slot = lax.broadcasted_iota(jnp.int32, shape, 0)
    lane = lax.broadcasted_iota(jnp.int32, shape, 1)
    cosine = jnp.broadcast_to(lat_ref[0:1, :], full)
    per_tile = LANES // RENORM
    growths, dampings, states = {}, {}, {}
    for group in groups:
        order = jnp.minimum(plan.order(group, slot, owners[group]), plan.degrees)
        order_value = order.astype(jnp.float32)
        for t in range(-(-plan.depth[group] // LANES)):
            step_int = lane + (t * LANES + 1)
            step = step_int.astype(jnp.float32)
            total = order_value + step
            growth = jnp.sqrt((4.0 * total * total - 1.0) / (step * (2.0 * order_value + step)))
            growth = jnp.where(order + step_int < plan.degrees, growth, 0.0)
            lower = (total - 1.0) * (total - 1.0)
            damping = jnp.sqrt(
                (step - 1.0) * (2.0 * order_value + step - 1.0) / jnp.maximum(4.0 * lower - 1.0, 1.0)
            )
            growths[group, t], dampings[group, t] = growth, growth * damping
        seed = seed_ref[group * GROUP : (group + 1) * GROUP, :]
        device = lax.broadcasted_iota(jnp.int32, seed.shape, 1)
        seed = jnp.sum(jnp.where(device == me, seed, 0.0), axis=1, keepdims=True)
        orders = order_value[:, 0:1]
        log_value = orders * lat_ref[1:2, :] + seed
        current = jnp.where(orders < plan.degrees, jnp.ones(full, jnp.float32), 0.0)
        states[group] = (current, jnp.zeros(full, jnp.float32), log_value)

    def one_span(t, active, i, carry):
        quadrature = jnp.broadcast_to(lat_ref[2:3, :], full)
        shift = lax.rem(LANES - i * RENORM, LANES)
        growth_tiles = [pltpu.roll(growths[group, t], shift, 1) for group in active]
        damping_tiles = [pltpu.roll(dampings[group, t], shift, 1) for group in active]
        factors = [jnp.exp(log_value) * quadrature for _, _, log_value in carry]
        now = [current for current, _, _ in carry]
        before = [previous for _, previous, _ in carry]
        values = [[[], []] for _ in active]
        for step in range(RENORM):
            for at, group in enumerate(active):
                parity = step % 2
                values[at][parity].append(now[at] * factors[at])
                growth = growth_tiles[at][:, step : step + 1]
                damping = damping_tiles[at][:, step : step + 1]
                following = (growth * cosine) * now[at] - damping * before[at]
                now[at], before[at] = following, now[at]
                if len(values[at][parity]) == 2:
                    row = plan.half_at[group] * GROUP + (t * per_tile + i) * (RENORM // 2 * GROUP)
                    row = pl.multiple_of(row + step // 4 * (2 * GROUP), 2 * GROUP)
                    top, low = split_parts(jnp.concatenate(values[at][parity], axis=0))
                    table_top[parity, pl.ds(row, 2 * GROUP), :] = top
                    table_low[parity, pl.ds(row, 2 * GROUP), :] = low
                    values[at][parity] = []
        out = []
        for at, (_, _, log_value) in enumerate(carry):
            largest = jnp.maximum(jnp.abs(now[at]), jnp.abs(before[at]))
            largest = jnp.where(largest == 0.0, 1.0, largest)
            inverse = 1.0 / largest
            out.append((now[at] * inverse, before[at] * inverse, log_value + jnp.log(largest)))
        return tuple(out)

    for t in range(-(-max(plan.depth[group] for group in groups) // LANES)):
        active = [group for group in groups if plan.depth[group] > t * LANES]
        count = min(min(per_tile, (plan.depth[group] - t * LANES) // RENORM) for group in active)
        carry = lax.fori_loop(0, count, functools.partial(one_span, t, active),
                              tuple(states[group] for group in active))
        for group, state in zip(active, carry):
            states[group] = state


def moved(tiles, start, width, dest):
    first, offset = start // LANES, start % LANES
    shift = (dest - offset) % LANES
    turn = lambda x: pltpu.roll(x, shift, 1) if shift else x
    value = turn(tiles[first])
    if offset + width > LANES:
        lane = lax.broadcasted_iota(jnp.int32, value.shape, 1)
        value = jnp.where(lane < dest + LANES - offset, value, turn(tiles[first + 1]))
    return value


def gather_fields(plan, group, sign, recv_ref, fold_top, fold_low):
    row, half_group = plan.row_at[group], plan.is_half(group)
    lane = lax.broadcasted_iota(jnp.int32, (GROUP, LANES), 1)
    width = plan.lat_rows
    for sy in range(plan.n_shell):
        for block in range(plan.blocks):
            sides = {}
            for inside in range(plan.per_block):
                band = block * plan.per_block + inside
                sources = [sy * plan.n_band + band, (sy + 1) * plan.n_band - 1 - band]
                if half_group:
                    sources = [sy * (plan.n_band // 2) + band]
                for side, source in enumerate(sources):
                    tiles = [
                        recv_ref[source, row + t * GROUP : row + (t + 1) * GROUP, :]
                        for t in range(plan.tiles)
                    ]
                    for piece in range(4 * plan.local_shells):
                        value = moved(tiles, piece * width, width, inside * width)
                        if inside:
                            value = jnp.where(lane < inside * width, sides[side, piece], value)
                        sides[side, piece] = value
            for field in range(2):
                for s in range(plan.local_shells):
                    pieces = [(p * 2 + field) * plan.local_shells + s for p in range(2)]
                    north = jnp.concatenate([sides[0, at] for at in pieces], axis=0)
                    if half_group:
                        folds = (north, sign * north)
                    else:
                        south = jnp.concatenate([sides[1, at] for at in pieces], axis=0)
                        folds = (north + south, north - south)
                    start = field * plan.columns + (sy * plan.local_shells + s) * 2 * GROUP
                    for parity, folded in enumerate(folds):
                        top, low = split_parts(folded)
                        at = (parity, pl.ds(start, 2 * GROUP), pl.ds(block * LANES, LANES))
                        fold_top[at] = top
                        fold_low[at] = low


def scatter_fields(plan, group, grids, send_ref):
    row, width = plan.row_at[group], plan.lat_rows
    lane = lax.broadcasted_iota(jnp.int32, (GROUP, LANES), 1)
    bands = plan.n_band // 2 if plan.is_half(group) else plan.n_band
    for sy in range(plan.n_shell):
        for band in range(bands):
            side = int(band >= plan.n_band // 2)
            mirrored = plan.n_band - 1 - band if side else band
            block, inside = mirrored // plan.per_block, mirrored % plan.per_block
            tiles = []
            for t in range(plan.tiles):
                tile = None
                for piece in range(4 * plan.local_shells):
                    start = piece * width - t * LANES
                    if start + width <= 0 or start >= LANES:
                        continue
                    p, field, s = piece // (2 * plan.local_shells), piece // plan.local_shells % 2, piece % plan.local_shells
                    at = ((sy * plan.local_shells + s) * 2 + p) * GROUP
                    value = grids[field][side][at : at + GROUP, pl.ds(block * LANES, LANES)]
                    shift = (start - inside * width) % LANES
                    if shift:
                        value = pltpu.roll(value, shift, 1)
                    tile = value if tile is None else jnp.where(lane < start, tile, value)
                tiles.append(tile)
            for t in range(plan.tiles):
                send_ref[sy * bands + band, row + t * GROUP : row + (t + 1) * GROUP, :] = tiles[t]


def degree_lanes(plan, group, owner, precision_ref, total, weight_ref, seen_ref):
    width = round_up(plan.groups * GROUP * plan.devices + plan.degrees, LANES)
    row = jnp.concatenate(
        [precision_ref[...].reshape(1, plan.degrees), jnp.zeros((1, width - plan.degrees), jnp.float32)], axis=1
    )
    row = jnp.broadcast_to(row, (GROUP, width))
    sub = lax.broadcasted_iota(jnp.int32, (GROUP, width), 0)
    precision = row
    for i in range(GROUP):
        start = plan.order(group, i, 0)
        precision = jnp.where(sub == i, pltpu.roll(row, (width - start) % width, 1), precision)
    precision = pltpu.roll(precision, lax.rem(width - owner, width), 1)
    copies = plan.columns // GROUP
    nothing = jnp.zeros((plan.columns - 2 * GROUP, LANES), jnp.float32)
    for t in range(plan.degree_tiles[group]):
        rows = pl.ds(plan.degree_at[group] + t * LANES, LANES)
        tile = precision[:, t * LANES : (t + 1) * LANES]
        weight_ref[rows, :] = jnp.concatenate([tile] * copies, axis=0).T
        tiles = []
        for p in range(2):
            at = plan.seen_at[group] + (p * plan.degree_tiles[group] + t) * GROUP
            tiles.append(total[at : at + GROUP, :])
        seen_ref[rows, :] = jnp.concatenate(tiles + [nothing], axis=0).T


class Misfit:
    def __init__(self, plan, group, owner, sign, log_ratio, seen_ref, weight_ref, table_top, table_low,
                 fold_top, fold_low):
        self.plan, self.group, self.sign, self.log_ratio = plan, group, sign, log_ratio
        self.seen_ref, self.weight_ref = seen_ref, weight_ref
        self.table_top, self.table_low = table_top, table_low
        self.fold_top, self.fold_low = fold_top, fold_low
        columns = self.columns = plan.columns
        half_depth = plan.depth[group] // 2
        chunk = max(c for c in range(RENORM // 2, 65, RENORM // 2) if half_depth % c == 0)
        self.chunk, self.chunks = chunk, half_depth // chunk
        self.lane = lax.broadcasted_iota(jnp.int32, (chunk, columns), 1)
        order = plan.order(group, lax.rem(self.lane, GROUP), owner)
        imaginary = lax.rem(self.lane // GROUP, 2) == 1
        self.keep = jnp.where((order == 0) & imaginary, 0.0, 1.0)
        self.offset = lax.broadcasted_iota(jnp.int32, (chunk, columns), 0) * 2 + order
        own_row = lax.broadcasted_iota(jnp.int32, (GROUP, columns), 0)
        own_lane = lax.rem(lax.broadcasted_iota(jnp.int32, (GROUP, columns), 1), GROUP)
        self.own = jnp.where(own_row == own_lane, 1.0, 0.0)

    def over_shells(self, x):
        shift = 2 * GROUP
        while shift < self.columns:
            x = x + pltpu.roll(x, shift, 1)
            shift *= 2
        return x

    def rows_at(self, c):
        size = self.chunk * GROUP
        start = self.plan.half_at[self.group] * GROUP + c * size
        return pl.ds(pl.multiple_of(start, size), size)

    def pick(self, values):
        return jnp.sum(values.reshape(self.chunk, GROUP, self.columns) * self.own[None], axis=1)

    def degrees_at(self, c, parity):
        start = self.plan.degree_at[self.group] + c * (2 * self.chunk) + parity
        return pl.ds(start, self.chunk, stride=2)

    def radial_at(self, c, parity):
        degree = self.offset + (c * (2 * self.chunk) + parity)
        return jnp.exp(degree.astype(jnp.float32) * self.log_ratio)

    def seen_at(self, c, parity):
        return self.seen_ref[self.degrees_at(c, parity), :]

    def weight_at(self, c, parity):
        return self.weight_ref[self.degrees_at(c, parity), :]

    def terms_of_both(self, c, parity):
        rows = self.rows_at(c)
        top = self.table_top[parity, rows, :]
        terms = (dot_abt(top, self.fold_top[parity]) + dot_abt(top, self.fold_low[parity])
                 + dot_abt(self.table_low[parity, rows, :], self.fold_top[parity]))
        return terms[:, : self.columns], terms[:, self.columns :]

    def fold_again(self, parity, folded):
        top, low = split_parts(folded)
        self.fold_top[parity, 0 : self.columns, :] = top
        self.fold_top[parity, self.columns : 2 * self.columns, :] = low

    def terms_again(self, c, parity):
        rows = self.rows_at(c)
        both = dot_abt(self.table_top[parity, rows, :], self.fold_top[parity])
        return (both[:, : self.columns] + both[:, self.columns :]
                + dot_abt(self.table_low[parity, rows, :], self.fold_top[parity, 0 : self.columns, :]))

    def adjoint(self, c, parity, weighted):
        rows = self.rows_at(c)
        wide = weighted[:, None, :] * self.own[None]
        top, low = split_parts(wide.reshape(self.chunk * GROUP, self.columns))
        both = dot_atb(jnp.concatenate([top, low], axis=1), self.table_top[parity, rows, :])
        return (both[: self.columns] + both[self.columns :]
                + dot_atb(top, self.table_low[parity, rows, :]))


def misfit_group(work, recv_ref, wanted_ref, grid_ref, send_ref):
    plan, group, chunk = work.plan, work.group, work.chunk
    gather_fields(plan, group, work.sign, recv_ref, work.fold_top, work.fold_low)

    def first_pass(c, carry):
        tall = pl.ds(pl.multiple_of(c * chunk, chunk), chunk)
        terms = [work.terms_of_both(c, parity) for parity in range(2)]
        for parity in range(2):
            radial, seen = work.radial_at(c, parity), work.seen_at(c, parity)
            first, ahead = (
                work.over_shells(work.pick(values) * radial - seen) for values in terms[parity]
            )
            wanted_ref[parity, tall, :] = ahead
            grid_ref[0, parity] += work.adjoint(c, parity, radial * work.weight_at(c, parity) * first)
        return carry

    def second_pass(c, carry):
        tall = pl.ds(pl.multiple_of(c * chunk, chunk), chunk)
        terms = [work.terms_again(c, parity) for parity in range(2)]
        for parity in range(2):
            radial = work.radial_at(c, parity)
            back = work.over_shells(work.pick(terms[parity]) * radial) * work.keep
            misfit = wanted_ref[parity, tall, :] - (0.5 * STEP * STEP) * back
            grid_ref[1, parity] += work.adjoint(c, parity, radial * work.weight_at(c, parity) * misfit)
        return carry

    grid_ref[...] = jnp.zeros_like(grid_ref)
    lax.fori_loop(0, work.chunks, first_pass, 0)
    for parity in range(2):
        work.fold_again(parity, 2.0 * grid_ref[0, parity])
    lax.fori_loop(0, work.chunks, second_pass, 0)

    for field in range(2):
        even, odd = grid_ref[field, 0], grid_ref[field, 1]
        grid_ref[field, 0] = even + odd
        grid_ref[field, 1] = even - odd
    grids = [[grid_ref.at[field, side] for side in range(2)] for field in range(2)]
    scatter_fields(plan, group, grids, send_ref)


def pack(work, values):
    packed = values[:GROUP]
    for block in range(1, work.chunk // GROUP):
        rows = values[block * GROUP : (block + 1) * GROUP]
        packed = jnp.where(work.lane[:GROUP] // (2 * GROUP) == block, rows, packed)
    return packed


def unpack(work, packed):
    blocks = []
    for block in range(work.chunk // GROUP):
        inside = work.lane[:GROUP] // (2 * GROUP) == block
        blocks.append(work.over_shells(jnp.where(inside, packed, 0.0)))
    return jnp.concatenate(blocks, axis=0)


def half_first(work, recv_ref, part_ref, swap_ref):
    gather_fields(work.plan, work.group, work.sign, recv_ref, work.fold_top, work.fold_low)
    for parity in range(2):
        radial = work.radial_at(0, parity)
        for field, values in enumerate(work.terms_of_both(0, parity)):
            part = work.over_shells(work.pick(values) * radial)
            at = 2 * field + parity
            part_ref[at] = part
            swap_ref[at * GROUP : (at + 1) * GROUP, :] = pack(work, part)


def half_second(work, part_ref, grid_ref, swap_ref, came_ref):
    grids = []
    for parity in range(2):
        seen = work.over_shells(work.seen_at(0, parity))
        first, ahead = (
            part_ref[at] + unpack(work, came_ref[at * GROUP : (at + 1) * GROUP, :]) - seen
            for at in (parity, 2 + parity)
        )
        part_ref[2 + parity] = ahead
        weighted = work.radial_at(0, parity) * work.weight_at(0, parity) * first
        grids.append(work.adjoint(0, parity, weighted))
    grid = grids[0] + work.sign * grids[1]
    grid_ref[0] = grid
    work.fold_again(0, grid)
    work.fold_again(1, work.sign * grid)
    for parity in range(2):
        part = work.over_shells(work.pick(work.terms_again(0, parity)) * work.radial_at(0, parity))
        part_ref[parity] = part
        swap_ref[parity * GROUP : (parity + 1) * GROUP, :] = pack(work, part)


def half_third(work, part_ref, grid_ref, came_ref, send_ref):
    grids = []
    for parity in range(2):
        back = part_ref[parity] + unpack(work, came_ref[parity * GROUP : (parity + 1) * GROUP, :])
        misfit = part_ref[2 + parity] - (0.5 * STEP * STEP) * back
        weighted = work.radial_at(0, parity) * work.weight_at(0, parity) * misfit
        grids.append(work.adjoint(0, parity, weighted))
    grid_ref[1] = grids[0] + work.sign * grids[1]
    scatter_fields(work.plan, work.group, [[grid_ref.at[0]], [grid_ref.at[1]]], send_ref)


def step_kernel(plan, density_ref, momentum_ref, place_ref, observed_ref, precision_ref,
                seed_ref, lat_ref, orders_ref, ratio_ref, top_hbm, low_hbm, total_ref, fourier_top,
                fourier_low, field_top, field_low, sent_ref, recv_ref, back_ref, out_ref,
                routed_ref, pair_ref, owned_ref, table_top, table_low, fold_top, fold_low, wanted_ref,
                grid_ref, weight_ref, seen_ref, part_ref, half_grid_ref, swap_ref, came_ref, load_sems,
                send_sem, recv_sem, back_send_sem, back_recv_sem, pair_sems, owned_sems, swap_sems):
    n, n_band = plan.devices, plan.n_band
    row, band = lax.axis_index("shell"), lax.axis_index("band")
    me = row * n_band + band
    south = (band >= n_band // 2).astype(jnp.int32)
    barrier = pltpu.get_barrier_semaphore()

    def peer(i):
        to = lax.rem(me + i, n)
        return to, (to // n_band, lax.rem(to, n_band))

    def greet(i, carry):
        pl.semaphore_signal(barrier, inc=1, device_id=peer(i)[1], device_id_type=MESH)
        return carry

    def rows_of(group):
        end = plan.row_at[group + 1] if group + 1 < plan.groups else plan.rows
        return pl.ds(plan.row_at[group], end - plan.row_at[group])

    owners = [me] * plan.groups
    if plan.halved:
        owners[-1] = row * (n_band // 2) + band + south * (n_band - 1 - 2 * band)

    def start_group(group, source, target, sent_sems, got_sems):
        rows, mine, count = rows_of(group), owners[group], plan.stride[group]
        bands = count // plan.n_shell
        turned = south if plan.is_half(group) else 0
        pltpu.make_async_copy(
            source.at[mine, rows], target.at[mine, rows], got_sems.at[group]
        ).start()

        def send(i, carry):
            to = lax.rem(mine + i, count)
            pltpu.make_async_remote_copy(
                src_ref=source.at[to, rows], dst_ref=target.at[mine, rows],
                send_sem=sent_sems.at[group], recv_sem=got_sems.at[group],
                device_id=(to // bands, turned * (n_band - 1) + (1 - 2 * turned) * lax.rem(to, bands)),
                device_id_type=MESH,
            ).start()
            return carry

        lax.fori_loop(1, count, send, 0)

    def wait_for(ref, sem):
        pltpu.make_async_copy(ref, ref, sem).wait()

    def load(group, part):
        source, target = ((top_hbm, fourier_top), (low_hbm, fourier_low))[part]
        rows = pl.ds(plan.table_at[group], GROUP * plan.stride[group])
        return pltpu.make_async_copy(source.at[:, rows], target.at[:, rows], load_sems.at[group, part])

    def fourier(group):
        rows = pl.ds(plan.table_at[group], GROUP * plan.stride[group])
        return fourier_top.at[:, rows], fourier_low.at[:, rows]

    for group in plan.sends:
        for part in range(2):
            load(group, part).start()
    lax.fori_loop(1, n, greet, 0)
    place_fields(plan, south, density_ref, momentum_ref, place_ref, field_top, field_low)

    core, place, places = lax.rem(band, 2), band // 2, n_band // 2
    pair_copy = pltpu.make_async_remote_copy(
        src_ref=routed_ref.at[:, 1 - core], dst_ref=pair_ref, send_sem=pair_sems.at[0],
        recv_sem=pair_sems.at[1], device_id=(row, band + 1 - 2 * core), device_id_type=MESH,
    )

    def hand_over(i, carry):
        to = lax.rem(place + i, places)
        pltpu.make_async_remote_copy(
            src_ref=pair_ref.at[to], dst_ref=owned_ref.at[place], send_sem=owned_sems.at[0],
            recv_sem=owned_sems.at[1], device_id=(row, 2 * to + core), device_id_type=MESH,
        ).start()
        return carry

    def share_observed():
        pair_copy.wait()
        pair_ref[...] += routed_ref[:, core]
        pltpu.make_async_copy(pair_ref.at[place], owned_ref.at[place], owned_sems.at[1]).start()
        lax.fori_loop(1, places, hand_over, 0)

    def rows_made(*groups):
        legendre(plan, groups, me, owners, seed_ref, lat_ref, table_top, table_low)

    def arrived(group):
        count = pl.ds(0, plan.stride[group])
        wait_for(recv_ref.at[count, rows_of(group)], recv_sem.at[group])

    sign = jnp.where(south == 1, -1.0, 1.0)
    last = plan.turns[0]
    full = plan.turns[1:] if plan.halved else plan.turns

    def log_ratios():
        lane = lax.broadcasted_iota(jnp.int32, (1, plan.columns), 1)
        ratio = jnp.ones((1, plan.columns), jnp.float32)
        for sy in range(plan.n_shell):
            for s in range(plan.local_shells):
                at = plan.ratio_row + s
                value = recv_ref[sy * (plan.stride[last] // plan.n_shell), at : at + 1, :]
                ratio = jnp.where(lane // (2 * GROUP) == sy * plan.local_shells + s, value, ratio)
        return jnp.log(ratio)

    def work_on(group):
        return Misfit(plan, group, owners[group], sign, log_ratio, seen_ref, weight_ref, table_top,
                      table_low, fold_top, fold_low)

    def swap(turn):
        count = (4, 2)[turn] * GROUP
        return pltpu.make_async_remote_copy(
            src_ref=swap_ref.at[turn, pl.ds(0, count)], dst_ref=came_ref.at[turn, pl.ds(0, count)],
            send_sem=swap_sems.at[turn, 0], recv_sem=swap_sems.at[turn, 1],
            device_id=(row, n_band - 1 - band), device_id_type=MESH,
        )

    for turn, group in enumerate(plan.sends):
        for part in range(2):
            load(group, part).wait()
        spectra(plan, group, field_top, field_low, *fourier(group), ratio_ref, sent_ref)
        if turn == 0:
            pl.semaphore_wait(barrier, n - 1)
        start_group(group, sent_ref, recv_ref, send_sem, recv_sem)
        if turn == 0:
            route_observed(plan, orders_ref, observed_ref, routed_ref)
            pair_copy.start()
        if turn == min(1, plan.groups - 1):
            share_observed()
        if turn == plan.groups - 1:
            rows_made(last)
            arrived(last)
            log_ratio = log_ratios()
            if plan.halved:
                half = work_on(last)
                half_first(half, recv_ref, part_ref, swap_ref.at[0])
                swap(0).start()

    if plan.groups > 1:
        rows_made(*plan.turns[1:])
    wait_for(owned_ref, owned_sems.at[1])
    owned = owned_ref[0]
    for z in range(1, places):
        owned = owned + owned_ref[z]
    owned_ref[0] = owned
    for group in range(plan.groups):
        degree_lanes(plan, group, owners[group], precision_ref, owned_ref.at[0], weight_ref, seen_ref)

    for group in full:
        if group != last:
            arrived(group)
        misfit_group(work_on(group), recv_ref, wanted_ref, grid_ref, back_ref)
        start_group(group, back_ref, out_ref, back_send_sem, back_recv_sem)
        if plan.halved and group == full[0]:
            swap(0).wait()
            half_second(half, part_ref, half_grid_ref, swap_ref.at[1], came_ref.at[0])
            swap(1).start()
    if plan.halved:
        swap(1).wait()
        half_third(half, part_ref, half_grid_ref, came_ref.at[1], back_ref)
        start_group(last, back_ref, out_ref, back_send_sem, back_recv_sem)

    total_ref[...] = jnp.zeros_like(total_ref)
    for group in full[:-1] + ([last] if plan.halved else []) + full[-1:]:
        count = pl.ds(0, plan.stride[group])
        wait_for(out_ref.at[count, rows_of(group)], back_recv_sem.at[group])
        add_grids(plan, group, out_ref, *fourier(group), total_ref)
    for group in range(plan.groups):
        rows, count = rows_of(group), pl.ds(0, plan.stride[group] - 1)
        wait_for(sent_ref.at[count, rows], send_sem.at[group])
        wait_for(back_ref.at[count, rows], back_send_sem.at[group])
    if places > 1:
        wait_for(pair_ref.at[pl.ds(0, places - 1)], owned_sems.at[0])


def step(plan, density, momentum, observed, precision, seed, orders, ratio):
    vmem = pl.BlockSpec(memory_space=pltpu.VMEM)
    smem = pl.BlockSpec(memory_space=pltpu.SMEM)
    hbm = pl.BlockSpec(memory_space=pl.ANY)
    fourier = [jnp.asarray(x) for x in plan.fourier()]
    placement = jnp.asarray(plan.placement())
    f32, bf16 = jnp.float32, jnp.bfloat16
    field = pltpu.VMEM((2, placement.shape[2], plan.lon_cells), bf16)
    chunks = pltpu.VMEM((plan.devices, plan.rows, LANES), f32)
    routed = pltpu.VMEM((plan.n_band // 2, 2, plan.seen_rows, LANES), f32)
    owned = pltpu.VMEM((plan.n_band // 2, plan.seen_rows, LANES), f32)
    table = pltpu.VMEM((2, plan.half_all * GROUP, plan.lat_lanes), bf16)
    fold = pltpu.VMEM((2, 2 * plan.columns, plan.lat_lanes), bf16)
    by_degree = pltpu.VMEM((plan.degree_all, plan.columns), f32)
    swap = pltpu.VMEM((2, 4 * GROUP, plan.columns), f32)
    sems = lambda *count: pltpu.SemaphoreType.DMA(count)
    return pl.pallas_call(
        functools.partial(step_kernel, plan),
        out_shape=jax.ShapeDtypeStruct((plan.wide, plan.lon_cells), f32),
        in_specs=[vmem] * 7 + [smem] * 2 + [hbm] * 2,
        out_specs=vmem,
        scratch_shapes=[pltpu.VMEM(fourier[0].shape, bf16)] * 2
        + [field] * 2 + [chunks] * 4
        + [routed, owned, owned, table, table, fold, fold,
           pltpu.VMEM((2, plan.depth[0] // 2, plan.columns), f32),
           pltpu.VMEM((2, 2, plan.columns, plan.lat_lanes), f32), by_degree, by_degree,
           pltpu.VMEM((4, plan.depth[-1] // 2, plan.columns), f32),
           pltpu.VMEM((2, plan.columns, plan.lat_lanes), f32), swap, swap]
        + [sems(plan.groups, 2)] + [sems(plan.groups)] * 4 + [sems(2)] * 2 + [sems(2, 2)],
        compiler_params=pltpu.CompilerParams(
            collective_id=0, has_side_effects=True, vmem_limit_bytes=VMEM_LIMIT
        ),
        name="step",
    )(density, momentum, placement, observed, precision, seed, jnp.asarray(plan.latitudes()),
      orders, ratio, *fourier)


def finish_kernel(plan, total_ref, turn_ref, density_ref, momentum_ref, new_density_ref, new_momentum_ref):
    south = (lax.axis_index("band") >= plan.n_band // 2).astype(jnp.int32)
    top, low = split_parts(total_ref[...])
    turn = turn_ref[south]
    grid = dot_ab(turn, top) + dot_ab(turn, low)
    density, momentum = density_ref[...], momentum_ref[...]
    half_momentum = momentum - 0.5 * STEP * (density + grid[: plan.cells])
    new_density = density + STEP * half_momentum
    new_density_ref[...] = new_density
    new_momentum_ref[...] = half_momentum - 0.5 * STEP * (new_density + grid[plan.cells :])


def finish(plan, total, density, momentum):
    turn = jnp.asarray(plan.turn().astype(ml_dtypes.bfloat16))
    wide = plan.lon_cells
    at_lanes = lambda rows: pl.BlockSpec((rows, wide), lambda i: (0, i))
    shape = jax.ShapeDtypeStruct(density.shape, jnp.float32)
    return pl.pallas_call(
        functools.partial(finish_kernel, plan),
        grid=(plan.lon_cells // wide,),
        in_specs=[at_lanes(plan.wide), pl.BlockSpec(turn.shape, lambda i: (0, 0, 0)),
                  at_lanes(plan.cells), at_lanes(plan.cells)],
        out_specs=[at_lanes(plan.cells)] * 2,
        out_shape=[shape, shape],
        compiler_params=pltpu.CompilerParams(vmem_limit_bytes=VMEM_LIMIT),
        name="finish",
    )(total, turn, density, momentum)


def body(density, momentum, observed, order_list, shell_ratio, precision):
    slots, _, degrees = observed.shape
    local_shells, lat_rows, lon_cells = density.shape
    n_shell, n_band = lax.axis_size("shell"), lax.axis_size("band")
    plan = Plan(n_shell, n_band, local_shells, lat_rows, lon_cells, degrees)
    order_value = jnp.asarray(plan.seed_orders())
    seed = 0.5 * (
        jnp.log(order_value + 0.5)
        + lax.lgamma(2.0 * order_value + 1.0)
        - order_value * jnp.log(4.0)
        - 2.0 * lax.lgamma(order_value + 1.0)
    )
    flat_density = density.reshape(plan.cells, lon_cells)
    flat_momentum = momentum.reshape(plan.cells, lon_cells)
    total = step(plan, flat_density, flat_momentum, observed, precision, seed, order_list, shell_ratio)
    new_density, new_momentum = finish(plan, total, flat_density, flat_momentum)
    return new_density.reshape(density.shape), new_momentum.reshape(density.shape)


def solution(mesh):
    in_specs = (
        P("shell", "band", None),
        P("shell", "band", None),
        P("band", None, None),
        P(),
        P("shell"),
        P(),
    )
    out_specs = (P("shell", "band", None), P("shell", "band", None))
    return jax.shard_map(body, mesh=mesh, in_specs=in_specs, out_specs=out_specs, check_vma=False)
```
